32 devices in a mesh: parts: 2 (over y), row: 4 (over z), col: 4 (over x, core).
Axes of the slice: x: 2, y: 2, z: 4, core: 2. Of those that a mesh axis runs over, the one named last changes fastest.
Arguments:
- embedding: float32 [32768, 128], P(('parts', 'row', 'col')), parts along dimension 0, may hold values from -1.8 to 1.8
- accumulator: float32 [32768, 128], P(('parts', 'row', 'col')), parts along dimension 0, may hold values from 0.1 to 1
- popularity: int32 [32768], P(('parts', 'row', 'col')), parts along dimension 0, may hold values from 1 to 64
- cooccur: bfloat16 [8, 4, 5, 256, 1024], P(('parts', 'row'), 'col'), parts along dimension 0, may hold values from 0 to 64, as said below
- pair_list: int32 [8, 4, 5, 3], P(('parts', 'row'), 'col'), parts along dimension 0, may hold values from 0 to 3, as said below
- live_count: int32 [8, 4], P(('parts', 'row'), 'col'), parts along dimension 0, may hold values from 0 to 5, as said below
Outputs:
- new_embedding: float32 [32768, 128], P(('parts', 'row', 'col')), parts along dimension 0
- new_accumulator: float32 [32768, 128], P(('parts', 'row', 'col')), parts along dimension 0
The draws below stay inside these ranges and needn't reach their ends.
There are 2 independent parts, one for each index of `parts`. The reference program is written for one: setup_inputs(seed, part) draws one part's arguments, and reference() takes and returns one part's arrays. A program takes and returns all parts, laid end to end along the dimension named above; each array names one. Nothing has to cross between parts.
Inputs may be any that keep to these rules, and one draw needn't show every extreme that they name: `pair_list`: slot s of holder (r, c) holds (a, b, h) with a < 4, b < 4, h < 4; in the first live_count[r, c] slots r + b < 4, the row block 4 r + a is at most the column block 4 (r + b) + c, and no triple repeats. Later slots are not read. `live_count`: holder (0, 3) lists 5; no holder lists more triples than it has that satisfy the conditions above. `cooccur`: each cell is 0 (not observed) or a weighted count of 1 or more.
All inputs are finite; a program needn't handle non-finite values.
Results may differ from the reference program's by a relative error of at most 0.0077.
Values may be sent and summed in bfloat16 or wider, within the bound.
No kernel may reach another device: no remote copies, remote signals or barrier semaphores. Data moves between devices by JAX's collectives and lax.ppermute only.
A program may use at most 128 MiB of HBM per device.

```python
import math
import jax
import jax.numpy as jnp
from jax import lax

D = 128
BLOCK = 1024
PIECE = 256
PAIRS_DEV = 5
WINDOW = 4
SPLIT = 4
ITEMS = 16384
N_ROW = 4
N_COL = 4


def pair_tables(key):
    candidates = N_COL * WINDOW * SPLIT
    flat_ids = jnp.arange(candidates)[None, None, :]
    row_ids = jnp.arange(N_ROW)[:, None, None]
    col_ids = jnp.arange(N_COL)[None, :, None]
    left_slot = flat_ids // (WINDOW * SPLIT)
    distance = flat_ids // SPLIT % WINDOW
    valid = jnp.logical_and(row_ids + distance < N_ROW, jnp.logical_or(distance > 0, left_slot <= col_ids))
    cand_count = jnp.sum(valid.astype(jnp.int32), axis=2)
    key_order, key_live = jax.random.split(key)
    subkeys = jax.random.split(key_order, N_ROW * N_COL)
    orders = jax.vmap(lambda subkey: jax.random.permutation(subkey, candidates))(subkeys).reshape(N_ROW, N_COL, candidates)
    scores = jnp.where(valid, orders, orders + candidates)
    picked = jnp.argsort(scores, axis=2, stable=True)[:, :, :PAIRS_DEV]
    triples = jnp.stack([picked // (WINDOW * SPLIT), picked // SPLIT % WINDOW, picked % SPLIT], axis=-1).astype(jnp.int32)
    wanted = jax.random.randint(key_live, (N_ROW, N_COL), 0, PAIRS_DEV + 1)
    live_rows = jnp.minimum(wanted, cand_count).astype(jnp.int32)
    live_rows = live_rows.at[0, N_COL - 1].set(PAIRS_DEV)
    return (triples, live_rows)


def draw_pair_list(key, part):
    return pair_tables(jax.random.fold_in(key, 11))[0]


def draw_live_count(key, part):
    return pair_tables(jax.random.fold_in(key, 11))[1]


def draw_cooccur(key, part):
    tile_shape = (N_ROW, N_COL, PAIRS_DEV, PIECE, BLOCK)
    key_mask, key_value = jax.random.split(jax.random.fold_in(key, 23))
    observed_share = 0.5
    values = jnp.exp(jax.random.uniform(key_value, tile_shape, jnp.float32, 0.0, math.log(64.0)))
    observed = jax.random.uniform(key_mask, tile_shape, jnp.float32) < observed_share
    return jnp.where(observed, values, 0.0).astype(jnp.float32).astype(jnp.bfloat16)


def plant(entries, rng, smallest, high):
    longest = entries.shape.index(max(entries.shape))
    spots = []
    for shift in (0, 1):
        where = [jax.random.randint(jax.random.fold_in(rng, axis), (), 0, length) for axis, length in enumerate(entries.shape)]
        where[longest] = (where[longest] + shift) % entries.shape[longest]
        spots.append(tuple(where))
    return entries.at[spots[0]].set(smallest).at[spots[1]].set(high)


def block_levels(key, extent, pieces, least, top_value):
    gain = 1.0
    for dim, parts in pieces:
        heights = jax.random.uniform(jax.random.fold_in(jax.random.fold_in(key, 6), dim), (parts,), jnp.float32, least / len(pieces), top_value / len(pieces))
        gain = gain * jnp.repeat(jnp.exp(heights), extent[dim] // parts).reshape((-1,) + (1,) * (len(extent) - 1 - dim))
    return gain


def noise(key, dims, width, limit, cuts=(), dtype=jnp.bfloat16):
    entries = jax.random.normal(key, dims, jnp.float32) * width
    if len(cuts) > 0:
        entries = block_levels(key, dims, cuts, -0.22, 0.18) * entries
    return jnp.clip(entries, min=-limit, max=limit).astype(dtype)


def setup_inputs(seed: int = 0, part: int = 0) -> dict:
    arg_keys = jax.random.split(jax.random.key(seed), 7)
    part_splits = jax.random.split(jax.random.fold_in(arg_keys[6], part), 7)
    return {
        "embedding": noise(part_splits[0], (ITEMS, D), 0.3, 1.8, ((0, 16),), jnp.float32),
        "accumulator": jnp.clip(jnp.exp(math.log(1.0) - 2.3025851 * jax.random.uniform(part_splits[1], (ITEMS, D), jnp.float32) ** block_levels(part_splits[1], (ITEMS, D), ((0, 16),), -0.2, 0.2)), 0.1, 1.0),
        "popularity": plant(jax.random.randint(part_splits[2], (ITEMS,), 1, 65), jax.random.fold_in(part_splits[2], 1), 1, 64).astype(jnp.int32),
        "cooccur": draw_cooccur(jax.random.fold_in(jax.random.fold_in(arg_keys[6], part), 71), part),
        "pair_list": draw_pair_list(jax.random.fold_in(jax.random.fold_in(arg_keys[6], part), 71), part),
        "live_count": draw_live_count(jax.random.fold_in(jax.random.fold_in(arg_keys[6], part), 71), part),
    }


LOG_SHIFT = 4.0
LEARN_RATE = 0.5

def tile_weights(counts_tile, row_piece, col_block, row_logs, col_logs, scale_root):
    scores = jnp.dot(row_piece, col_block.T, preferred_element_type=jnp.float32)
    count_values = counts_tile.astype(jnp.float32)
    observed = count_values > 0
    target = jnp.log(jnp.maximum(count_values, 1.0)) - row_logs.astype(jnp.float32)[:, None] - col_logs.astype(jnp.float32)[None, :] + LOG_SHIFT
    confidence = 0.1 + 0.25 * jnp.sqrt(count_values)
    misfit = scores - target
    slopes = jnp.where(observed, confidence * misfit, jax.nn.sigmoid(misfit))
    return (slopes / scale_root).astype(jnp.bfloat16)

def reference(embedding, accumulator, popularity, cooccur, pair_list, live_count):
    vectors = embedding.astype(jnp.bfloat16).reshape(N_ROW, N_COL, BLOCK, D)
    log_pop = jnp.log(popularity.astype(jnp.float32)).astype(jnp.bfloat16).reshape(N_ROW, N_COL, BLOCK)
    padded_vecs = jnp.concatenate([vectors, jnp.zeros((WINDOW, N_COL, BLOCK, D), jnp.bfloat16)], axis=0)
    padded_logs = jnp.concatenate([log_pop, jnp.zeros((WINDOW, N_COL, BLOCK), jnp.bfloat16)], axis=0)
    scale_root = math.sqrt(BLOCK)
    anchor = jnp.zeros((), jnp.int32)

    def holder(holder_index, gradient):
        row_pos = (holder_index // N_COL).astype(jnp.int32)
        col_pos = (holder_index % N_COL).astype(jnp.int32)

        def one_tile(slot_index, totals):
            row_slot = pair_list[row_pos, col_pos, slot_index, 0].astype(jnp.int32)
            distance = pair_list[row_pos, col_pos, slot_index, 1].astype(jnp.int32)
            part_index = pair_list[row_pos, col_pos, slot_index, 2].astype(jnp.int32)
            first = (part_index * PIECE).astype(jnp.int32)
            far_row = (row_pos + distance).astype(jnp.int32)
            row_piece = lax.dynamic_slice(vectors, (row_pos, row_slot, first, anchor), (1, 1, PIECE, D)).reshape(PIECE, D)
            row_logs = lax.dynamic_slice(log_pop, (row_pos, row_slot, first), (1, 1, PIECE)).reshape(PIECE)
            col_block = lax.dynamic_slice(padded_vecs, (far_row, col_pos, anchor, anchor), (1, 1, BLOCK, D)).reshape(BLOCK, D)
            col_logs = lax.dynamic_slice(padded_logs, (far_row, col_pos, anchor), (1, 1, BLOCK)).reshape(BLOCK)
            weights = tile_weights(cooccur[row_pos, col_pos, slot_index], row_piece, col_block, row_logs, col_logs, scale_root)
            left_piece = jnp.dot(weights, col_block, preferred_element_type=jnp.float32)
            right_block = jnp.dot(weights.T, row_piece, preferred_element_type=jnp.float32)
            current = lax.dynamic_slice(totals, (row_pos, row_slot, first, anchor), (1, 1, PIECE, D))
            totals = lax.dynamic_update_slice(totals, current + left_piece[None, None], (row_pos, row_slot, first, anchor))
            current = lax.dynamic_slice(totals, (far_row, col_pos, anchor, anchor), (1, 1, BLOCK, D))
            totals = lax.dynamic_update_slice(totals, current + right_block[None, None], (far_row, col_pos, anchor, anchor))
            return totals
        return lax.fori_loop(jnp.zeros((), jnp.int32), live_count[row_pos, col_pos].astype(jnp.int32), one_tile, gradient)
    gradient = lax.fori_loop(0, N_ROW * N_COL, holder, jnp.zeros((N_ROW + WINDOW, N_COL, BLOCK, D), jnp.float32))
    gradient = gradient[:N_ROW].reshape(ITEMS, D)
    new_accumulator = accumulator + gradient * gradient
    new_embedding = embedding - LEARN_RATE * gradient / jnp.sqrt(new_accumulator)
    return (new_embedding, new_accumulator)
```

```python
import functools
import math

import jax
import jax.numpy as jnp
from jax import lax
from jax.experimental import pallas as pl
from jax.experimental.pallas import tpu as pltpu
from jax.sharding import PartitionSpec as P

LOG_SHIFT = 4.0
LEARN_RATE = 0.5
LANES = 128
LOG_ROWS = 16
CHUNK = 256
MIB = 1 << 20


def shifted(array, axis, by):
    count = lax.axis_size(axis)
    pairs = [(i, i + by) for i in range(count) if 0 <= i + by < count]
    return lax.ppermute(array, axis, pairs)


def flipped(array, axis, bit):
    count = lax.axis_size(axis)
    return lax.ppermute(array, axis, [(i, i ^ bit) for i in range(count)])


def pack_kernel(embedding, popularity, message):
    items = embedding.shape[0]
    message[:items] = embedding[...].astype(jnp.bfloat16)
    logs = jnp.log(popularity[...].astype(jnp.float32))
    message[items:] = jnp.concatenate([logs, jnp.zeros_like(logs)], axis=0).astype(jnp.bfloat16)


def pack(embedding, popularity):
    items, dim = embedding.shape
    return pl.pallas_call(
        pack_kernel,
        out_shape=jax.ShapeDtypeStruct((items + LOG_ROWS, dim), jnp.bfloat16),
        in_specs=[pl.BlockSpec(memory_space=pltpu.VMEM)] * 2,
        out_specs=pl.BlockSpec(memory_space=pltpu.VMEM),
        compiler_params=pltpu.CompilerParams(vmem_limit_bytes=4 * MIB),
    )(embedding, popularity.reshape(items // LANES, LANES))


def tile_kernel(distance, n_col, n_prev, *refs):
    refs = list(refs)
    take = lambda count: [refs.pop(0) for _ in range(count)]
    live, pairs, cooccur = take(3)
    row_refs = take(n_col)
    (window,) = take(1)
    prev = take(n_prev)
    last = n_prev > 0
    (right_out,) = take(1)
    left_outs = take(2 if last else 1)
    tiles, row_vecs, row_logs, right_acc = take(4)
    if last:
        left_acc, pieces = take(2)
    tile_sem, vec_sem, log_sem = take(3)
    if last:
        (piece_sem,) = take(1)
    slots, piece_rows, items = tiles.shape
    me = lax.axis_index("col")
    n_live = live[0, 0]
    scale = 1.0 / math.sqrt(items)

    def listed(slot):
        return jnp.logical_and(slot < n_live, pairs[0, 0, slot, 1] == distance)

    def tile_copy(slot):
        return pltpu.make_async_copy(cooccur.at[0, 0, slot], tiles.at[slot], tile_sem.at[slot])

    def row_copies(slot, source):
        first = pl.multiple_of(pairs[0, 0, slot, 2] * piece_rows, piece_rows)
        return (
            pltpu.make_async_copy(
                source.at[pl.ds(first, piece_rows)], row_vecs.at[slot], vec_sem.at[slot]
            ),
            pltpu.make_async_copy(
                source.at[pl.ds(items, LOG_ROWS)], row_logs.at[slot], log_sem.at[slot]
            ),
        )

    def piece_copy(slot, source):
        return pltpu.make_async_copy(source.at[slot], pieces.at[slot], piece_sem.at[slot])

    for slot in range(slots):

        @pl.when(listed(slot))
        def _():
            tile_copy(slot).start()
            place = jnp.bitwise_xor(pairs[0, 0, slot, 0], me)
            for index in range(n_col):

                @pl.when(place == index)
                def _():
                    for copy in row_copies(slot, row_refs[index]):
                        copy.start()

        if last:
            for index in range(n_prev):

                @pl.when(jnp.logical_and(slot < n_live, pairs[0, 0, slot, 1] == index))
                def _():
                    piece_copy(slot, prev[index]).start()

    right_acc[...] = jnp.zeros_like(right_acc)
    if last:
        left_acc[...] = jnp.zeros_like(left_acc)

    def add_left(slot, value):
        place = jnp.bitwise_xor(pairs[0, 0, slot, 0], me)
        first = place * items + pairs[0, 0, slot, 2] * piece_rows
        view = pl.ds(pl.multiple_of(first, piece_rows), piece_rows)
        left_acc[view, :] += value

    def one_tile(slot):
        tile_copy(slot).wait()
        for copy in row_copies(slot, row_refs[0]):
            copy.wait()
        piece = row_vecs[slot]
        piece_t = piece.T
        group = pairs[0, 0, slot, 2] * (piece_rows // LANES)
        logs = row_logs[slot]
        places = lax.broadcasted_iota(jnp.int32, (LOG_ROWS, LANES), 0)
        log_rows = []
        for part in range(piece_rows // LANES):
            chosen = jnp.where(places == group + part, 1.0, 0.0).astype(jnp.bfloat16)
            log_rows.append(
                lax.dot_general(
                    logs, chosen, (((0,), (0,)), ((), ())), preferred_element_type=jnp.float32
                )
            )
        row_term = jnp.concatenate(log_rows, axis=0) - LOG_SHIFT
        row_term = jnp.concatenate([row_term] * (CHUNK // LANES), axis=1)
        col_logs = window[items:, :].astype(jnp.float32)
        left = jnp.zeros((piece_rows, piece.shape[1]), jnp.float32)
        for chunk in range(items // CHUNK):
            cols = slice(chunk * CHUNK, (chunk + 1) * CHUNK)
            block = window[cols, :]
            per = CHUNK // LANES
            col_term = jnp.concatenate(
                [col_logs[chunk * per + i : chunk * per + i + 1] for i in range(per)], axis=1
            )
            scores = lax.dot_general(
                piece, block, (((1,), (1,)), ((), ())), preferred_element_type=jnp.float32
            )
            count = tiles[slot, :, cols].astype(jnp.float32)
            clipped = jnp.maximum(count, 1.0)
            misfit = (scores + row_term) + (col_term - jnp.log(clipped))
            root = clipped * lax.rsqrt(clipped)
            seen = (0.1 * scale + (0.25 * scale) * root) * misfit
            unseen = (0.5 * scale) * jnp.tanh(0.5 * misfit) + 0.5 * scale
            weights = jnp.where(count > 0, seen, unseen).astype(jnp.bfloat16)
            left = left + jnp.dot(weights, block, preferred_element_type=jnp.float32)
            right_acc[:, cols] += jnp.dot(piece_t, weights, preferred_element_type=jnp.float32)
        if last:
            add_left(slot, left)
        else:
            left_outs[0][slot] = left

    @pl.loop(0, slots)
    def _(slot):
        @pl.when(listed(slot))
        def _():
            one_tile(slot)

    right_out[...] = right_acc[...].T.astype(right_out.dtype)
    if last:

        @pl.loop(0, slots)
        def _(slot):
            @pl.when(jnp.logical_and(slot < n_live, jnp.logical_not(listed(slot))))
            def _():
                piece_copy(slot, prev[0]).wait()
                add_left(slot, pieces[slot])

        for index in range(n_col):
            block = left_acc[index * items : (index + 1) * items, :]
            if index % 2:
                left_outs[0][index // 2] = block.astype(jnp.bfloat16)
            else:
                left_outs[1][index // 2] = block


def run_tiles(distance, live, pairs, cooccur, rows, window, prev):
    _, _, slots, piece_rows, items = cooccur.shape
    dim = window.shape[1]
    n_col = len(rows)
    any_spec = pl.BlockSpec(memory_space=pl.ANY)
    vmem_spec = pl.BlockSpec(memory_space=pltpu.VMEM)
    smem_spec = pl.BlockSpec(memory_space=pltpu.SMEM)
    right = jax.ShapeDtypeStruct((items, dim), jnp.bfloat16 if distance else jnp.float32)
    scratch = [
        pltpu.VMEM((slots, piece_rows, items), jnp.bfloat16),
        pltpu.VMEM((slots, piece_rows, dim), jnp.bfloat16),
        pltpu.VMEM((slots, LOG_ROWS, dim), jnp.bfloat16),
        pltpu.VMEM((dim, items), jnp.float32),
    ]
    sems = [pltpu.SemaphoreType.DMA((slots,))] * 3
    if prev:
        outs = (
            right,
            jax.ShapeDtypeStruct((n_col // 2, items, dim), jnp.bfloat16),
            jax.ShapeDtypeStruct((n_col // 2, items, dim), jnp.float32),
        )
        scratch += [
            pltpu.VMEM((n_col * items, dim), jnp.float32),
            pltpu.VMEM((slots, piece_rows, dim), jnp.float32),
        ]
        sems += [pltpu.SemaphoreType.DMA((slots,))]
    else:
        outs = (right, jax.ShapeDtypeStruct((slots, piece_rows, dim), jnp.float32))
    return pl.pallas_call(
        functools.partial(tile_kernel, distance, n_col, len(prev)),
        out_shape=outs,
        in_specs=[smem_spec] * 2
        + [any_spec]
        + [any_spec] * n_col
        + [vmem_spec]
        + [any_spec] * len(prev),
        out_specs=tuple(vmem_spec for _ in outs),
        scratch_shapes=scratch + sems,
        compiler_params=pltpu.CompilerParams(vmem_limit_bytes=32 * MIB),
        cost_estimate=pl.CostEstimate(
            flops=2 * 3 * piece_rows * items * dim * 2,
            bytes_accessed=4 * MIB,
            transcendentals=3 * 2 * piece_rows * items,
        ),
    )(live, pairs, cooccur, *rows, window, *prev)


def shards(embedding, accumulator, popularity, cooccur, pair_list, live_count):
    items = embedding.shape[0]
    n_col = lax.axis_size("col")
    message = pack(embedding, popularity)
    reach = min(8, lax.axis_size("row"))
    rows = {0: message}
    bit = n_col // 2
    while bit:
        rows.update({place ^ bit: flipped(block, "col", bit) for place, block in list(rows.items())})
        bit //= 2
    row_list = [rows[place] for place in range(n_col)]
    windows = [message] + [shifted(message, "row", -distance) for distance in range(1, reach)]
    prev = []
    right = []
    for distance in range(reach):
        done = run_tiles(
            distance,
            live_count,
            pair_list,
            cooccur,
            row_list,
            windows[distance],
            prev if distance == reach - 1 else [],
        )
        prev.append(done[1])
        right.append(done[0])
    gradient = right[0]
    for distance in range(1, reach):
        gradient = gradient + shifted(right[distance], "row", distance).astype(jnp.float32)
    send, keep = done[1], done[2]
    keep = [keep[place] for place in range(n_col // 2)]
    got = flipped(send, "col", 1)
    keep = [mine + got[place].astype(jnp.float32) for place, mine in enumerate(keep)]
    bit = 2
    while bit < n_col:
        sent = [keep[place].astype(jnp.bfloat16) for place in range(1, len(keep), 2)]
        keep = [
            keep[2 * place] + flipped(block, "col", bit).astype(jnp.float32)
            for place, block in enumerate(sent)
        ]
        bit *= 2
    gradient = gradient + keep[0]
    new_accumulator = accumulator + gradient * gradient
    new_embedding = embedding - LEARN_RATE * gradient / jnp.sqrt(new_accumulator)
    return (new_embedding, new_accumulator)


def solution(mesh):
    in_specs = (
        P(("parts", "row", "col"), None),
        P(("parts", "row", "col"), None),
        P(("parts", "row", "col")),
        P(("parts", "row"), "col", None, None, None),
        P(("parts", "row"), "col", None, None),
        P(("parts", "row"), "col"),
    )
    out_specs = (P(("parts", "row", "col"), None), P(("parts", "row", "col"), None))
    return jax.shard_map(shards, mesh=mesh, in_specs=in_specs, out_specs=out_specs, check_vma=False)
```

```python
import functools
import math

import jax
import jax.numpy as jnp
from jax import lax
from jax.experimental import pallas as pl
from jax.experimental.pallas import tpu as pltpu
from jax.sharding import PartitionSpec as P

LOG_SHIFT = 4.0
LEARN_RATE = 0.5
LANES = 128
LOG_ROWS = 16
CHUNK = 256
MIB = 1 << 20
PARTS = 2


def shifted(array, axis, by):
    count = lax.axis_size(axis)
    pairs = [(i, i + by) for i in range(count) if 0 <= i + by < count]
    return lax.ppermute(array, axis, pairs)


def flipped(array, axis, bit):
    count = lax.axis_size(axis)
    return lax.ppermute(array, axis, [(i, i ^ bit) for i in range(count)])


def pack_kernel(embedding, popularity, message):
    items = embedding.shape[0]
    message[:items] = embedding[...].astype(jnp.bfloat16)
    logs = jnp.log(popularity[...].astype(jnp.float32))
    message[items:] = jnp.concatenate([logs, jnp.zeros_like(logs)], axis=0).astype(jnp.bfloat16)


def pack(embedding, popularity):
    items, dim = embedding.shape
    return pl.pallas_call(
        pack_kernel,
        out_shape=jax.ShapeDtypeStruct((items + LOG_ROWS, dim), jnp.bfloat16),
        in_specs=[pl.BlockSpec(memory_space=pltpu.VMEM)] * 2,
        out_specs=pl.BlockSpec(memory_space=pltpu.VMEM),
        compiler_params=pltpu.CompilerParams(vmem_limit_bytes=4 * MIB),
    )(embedding, popularity.reshape(items // LANES, LANES))


def fetch_kernel(live, cooccur, after, tiles, sem):
    del after
    slots = tiles.shape[0]
    n_live = live[0, 0]

    def tile_copy(slot):
        return pltpu.make_async_copy(cooccur.at[0, 0, slot], tiles.at[slot], sem.at[slot])

    for slot in range(slots):

        @pl.when(slot < n_live)
        def _():
            tile_copy(slot).start()

    for slot in range(slots):

        @pl.when(slot < n_live)
        def _():
            tile_copy(slot).wait()


def fetch(live, cooccur, after):
    _, _, slots, piece_rows, items = cooccur.shape
    return pl.pallas_call(
        fetch_kernel,
        out_shape=jax.ShapeDtypeStruct((slots, piece_rows, items), cooccur.dtype),
        in_specs=[
            pl.BlockSpec(memory_space=pltpu.SMEM),
            pl.BlockSpec(memory_space=pltpu.HBM),
            pl.BlockSpec(memory_space=pl.ANY),
        ],
        out_specs=pl.BlockSpec(memory_space=pltpu.VMEM),
        scratch_shapes=[pltpu.SemaphoreType.DMA((slots,))],
        compiler_params=pltpu.CompilerParams(vmem_limit_bytes=8 * MIB),
    )(live, cooccur, after)


def tile_kernel(distance, n_col, earlier, last, *refs):
    refs = list(refs)
    take = lambda count: [refs.pop(0) for _ in range(count)]
    live, pairs, tiles = take(3)
    row_refs = take(n_col)
    (window,) = take(1)
    prev = take(len(earlier))
    (right_out,) = take(1)
    left_outs = take(2 if last else 1)
    row_vecs, row_logs, right_acc = take(3)
    if last:
        left_acc, pieces = take(2)
    vec_sem, log_sem = take(2)
    if last:
        (piece_sem,) = take(1)
    slots, piece_rows, items = tiles.shape
    me = lax.axis_index("col")
    n_live = live[0, 0]
    scale = 1.0 / math.sqrt(items)

    def listed(slot):
        return jnp.logical_and(slot < n_live, pairs[0, 0, slot, 1] == distance)

    def row_copies(slot, source):
        first = pl.multiple_of(pairs[0, 0, slot, 2] * piece_rows, piece_rows)
        return (
            pltpu.make_async_copy(
                source.at[pl.ds(first, piece_rows)], row_vecs.at[slot], vec_sem.at[slot]
            ),
            pltpu.make_async_copy(
                source.at[pl.ds(items, LOG_ROWS)], row_logs.at[slot], log_sem.at[slot]
            ),
        )

    def piece_copy(slot, source):
        return pltpu.make_async_copy(source.at[slot], pieces.at[slot], piece_sem.at[slot])

    for slot in range(slots):

        @pl.when(listed(slot))
        def _():
            place = jnp.bitwise_xor(pairs[0, 0, slot, 0], me)
            for index in range(n_col):

                @pl.when(place == index)
                def _():
                    for copy in row_copies(slot, row_refs[index]):
                        copy.start()

        if last:
            for source, index in zip(prev, earlier):

                @pl.when(jnp.logical_and(slot < n_live, pairs[0, 0, slot, 1] == index))
                def _():
                    piece_copy(slot, source).start()

    right_acc[...] = jnp.zeros_like(right_acc)
    if last:
        left_acc[...] = jnp.zeros_like(left_acc)

    def add_left(slot, value):
        place = jnp.bitwise_xor(pairs[0, 0, slot, 0], me)
        first = place * items + pairs[0, 0, slot, 2] * piece_rows
        view = pl.ds(pl.multiple_of(first, piece_rows), piece_rows)
        left_acc[view, :] += value

    def one_tile(slot):
        for copy in row_copies(slot, row_refs[0]):
            copy.wait()
        piece = row_vecs[slot]
        piece_t = piece.T
        group = pairs[0, 0, slot, 2] * (piece_rows // LANES)
        logs = row_logs[slot]
        places = lax.broadcasted_iota(jnp.int32, (LOG_ROWS, LANES), 0)
        log_rows = []
        for part in range(piece_rows // LANES):
            chosen = jnp.where(places == group + part, 1.0, 0.0).astype(jnp.bfloat16)
            log_rows.append(
                lax.dot_general(
                    logs, chosen, (((0,), (0,)), ((), ())), preferred_element_type=jnp.float32
                )
            )
        row_term = jnp.concatenate(log_rows, axis=0) - LOG_SHIFT
        row_term = jnp.concatenate([row_term] * (CHUNK // LANES), axis=1)
        col_logs = window[items:, :].astype(jnp.float32)
        left = jnp.zeros((piece_rows, piece.shape[1]), jnp.float32)
        for chunk in range(items // CHUNK):
            cols = slice(chunk * CHUNK, (chunk + 1) * CHUNK)
            block = window[cols, :]
            per = CHUNK // LANES
            col_term = jnp.concatenate(
                [col_logs[chunk * per + i : chunk * per + i + 1] for i in range(per)], axis=1
            )
            scores = lax.dot_general(
                piece, block, (((1,), (1,)), ((), ())), preferred_element_type=jnp.float32
            )
            count = tiles[slot, :, cols].astype(jnp.float32)
            clipped = jnp.maximum(count, 1.0)
            misfit = (scores + row_term) + (col_term - jnp.log(clipped))
            root = clipped * lax.rsqrt(clipped)
            seen = (0.1 * scale + (0.25 * scale) * root) * misfit
            unseen = (0.5 * scale) * jnp.tanh(0.5 * misfit) + 0.5 * scale
            weights = jnp.where(count > 0, seen, unseen).astype(jnp.bfloat16)
            left = left + jnp.dot(weights, block, preferred_element_type=jnp.float32)
            right_acc[:, cols] += jnp.dot(piece_t, weights, preferred_element_type=jnp.float32)
        if last:
            add_left(slot, left)
        else:
            left_outs[0][slot] = left

    @pl.loop(0, slots)
    def _(slot):
        @pl.when(listed(slot))
        def _():
            one_tile(slot)

    right_out[...] = right_acc[...].T.astype(right_out.dtype)
    if last:

        @pl.loop(0, slots)
        def _(slot):
            @pl.when(jnp.logical_and(slot < n_live, jnp.logical_not(listed(slot))))
            def _():
                piece_copy(slot, prev[0]).wait()
                add_left(slot, pieces[slot])

        for index in range(n_col):
            block = left_acc[index * items : (index + 1) * items, :]
            if index % 2:
                left_outs[0][index // 2] = block.astype(jnp.bfloat16)
            else:
                left_outs[1][index // 2] = block


def run_tiles(distance, live, pairs, tiles, rows, window, earlier, last, dtype):
    slots, piece_rows, items = tiles.shape
    dim = window.shape[1]
    n_col = len(rows)
    any_spec = pl.BlockSpec(memory_space=pl.ANY)
    vmem_spec = pl.BlockSpec(memory_space=pltpu.VMEM)
    smem_spec = pl.BlockSpec(memory_space=pltpu.SMEM)
    right = jax.ShapeDtypeStruct((items, dim), dtype)
    scratch = [
        pltpu.VMEM((slots, piece_rows, dim), jnp.bfloat16),
        pltpu.VMEM((slots, LOG_ROWS, dim), jnp.bfloat16),
        pltpu.VMEM((dim, items), jnp.float32),
    ]
    sems = [pltpu.SemaphoreType.DMA((slots,))] * 2
    if last:
        outs = (
            right,
            jax.ShapeDtypeStruct((n_col // 2, items, dim), jnp.bfloat16),
            jax.ShapeDtypeStruct((n_col // 2, items, dim), jnp.float32),
        )
        scratch += [
            pltpu.VMEM((n_col * items, dim), jnp.float32),
            pltpu.VMEM((slots, piece_rows, dim), jnp.float32),
        ]
        sems += [pltpu.SemaphoreType.DMA((slots,))]
    else:
        outs = (right, jax.ShapeDtypeStruct((slots, piece_rows, dim), jnp.float32))
    return pl.pallas_call(
        functools.partial(tile_kernel, distance, n_col, tuple(earlier), last),
        out_shape=outs,
        in_specs=[smem_spec] * 2
        + [vmem_spec]
        + [any_spec] * n_col
        + [vmem_spec]
        + [any_spec] * len(earlier),
        out_specs=tuple(vmem_spec for _ in outs),
        scratch_shapes=scratch + sems,
        compiler_params=pltpu.CompilerParams(vmem_limit_bytes=24 * MIB),
    )(live, pairs, tiles, *rows, window, *earlier.values())


def shards(embedding, accumulator, popularity, cooccur, pair_list, live_count):
    items = embedding.shape[0]
    n_col = lax.axis_size("col")
    message = pack(embedding, popularity)
    reach = min(8, lax.axis_size("row"))
    windows = {0: message, 1: shifted(message, "row", -1)}
    if reach == 4:
        windows[3] = shifted(message, "row", -3)
        below = lax.ppermute(message, "row", [(3, 1)])
    rows = [message] + [flipped(message, "col", place) for place in range(1, n_col)]
    if reach == 4:
        windows[2] = below + lax.ppermute(windows[1], "row", [(1, 0)])
    else:
        for distance in range(2, reach):
            windows[distance] = shifted(message, "row", -distance)
    tiles = fetch(live_count, cooccur, rows[1])
    right, earlier = {}, {}
    order = [reach - 1, 0, 1, *range(2, reach - 1)]
    for distance in order:
        done = run_tiles(
            distance,
            live_count,
            pair_list,
            tiles,
            rows,
            windows[distance],
            earlier,
            distance == order[-1],
            jnp.bfloat16 if distance == reach - 1 else jnp.float32,
        )
        right[distance], earlier[distance] = done[:2]
    passed = jnp.split(shifted(right[reach - 1], "row", 1), PARTS)
    for distance in range(reach - 2, 0, -1):
        terms = jnp.split(right[distance], PARTS)
        terms = [(a + b.astype(jnp.float32)).astype(jnp.bfloat16) for a, b in zip(terms, passed)]
        passed = [shifted(term, "row", 1) for term in terms]
    gradient = right[0] + jnp.concatenate(passed).astype(jnp.float32)
    send, keep = done[1], done[2]
    keep = [keep[place] for place in range(n_col // 2)]
    got = flipped(send, "col", 1)
    keep = [mine + got[place].astype(jnp.float32) for place, mine in enumerate(keep)]
    bit = 2
    while bit < n_col:
        sent = [keep[place].astype(jnp.bfloat16) for place in range(1, len(keep), 2)]
        keep = [
            keep[2 * place] + flipped(block, "col", bit).astype(jnp.float32)
            for place, block in enumerate(sent)
        ]
        bit *= 2
    gradient = gradient + keep[0]
    new_accumulator = accumulator + gradient * gradient
    new_embedding = embedding - LEARN_RATE * gradient / jnp.sqrt(new_accumulator)
    return (new_embedding, new_accumulator)


def solution(mesh):
    in_specs = (
        P(("parts", "row", "col"), None),
        P(("parts", "row", "col"), None),
        P(("parts", "row", "col")),
        P(("parts", "row"), "col", None, None, None),
        P(("parts", "row"), "col", None, None),
        P(("parts", "row"), "col"),
    )
    out_specs = (P(("parts", "row", "col"), None), P(("parts", "row", "col"), None))
    return jax.shard_map(shards, mesh=mesh, in_specs=in_specs, out_specs=out_specs, check_vma=False)
```

```python
import functools
import math

import jax
import jax.numpy as jnp
from jax import lax
from jax.experimental import pallas as pl
from jax.experimental.pallas import tpu as pltpu
from jax.sharding import PartitionSpec as P

LOG_SHIFT = 4.0
LEARN_RATE = 0.5
LANES = 128
LOG_ROWS = 16
CHUNK = 1024
MIB = 1 << 20
PARTS = 2


def shifted(array, axis, by):
    count = lax.axis_size(axis)
    pairs = [(i, i + by) for i in range(count) if 0 <= i + by < count]
    return lax.ppermute(array, axis, pairs)


def flipped(array, axis, bit):
    count = lax.axis_size(axis)
    return lax.ppermute(array, axis, [(i, i ^ bit) for i in range(count)])


def pack_kernel(embedding, popularity, message):
    items = embedding.shape[0]
    message[:items] = embedding[...].astype(jnp.bfloat16)
    logs = jnp.log(popularity[...].astype(jnp.float32))
    message[items:] = jnp.concatenate([logs, jnp.zeros_like(logs)], axis=0).astype(jnp.bfloat16)


def pack(embedding, popularity):
    items, dim = embedding.shape
    return pl.pallas_call(
        pack_kernel,
        out_shape=jax.ShapeDtypeStruct((items + LOG_ROWS, dim), jnp.bfloat16),
        in_specs=[pl.BlockSpec(memory_space=pltpu.VMEM)] * 2,
        out_specs=pl.BlockSpec(memory_space=pltpu.VMEM),
        compiler_params=pltpu.CompilerParams(vmem_limit_bytes=4 * MIB),
    )(embedding, popularity.reshape(items // LANES, LANES))


def fetch_kernel(live, cooccur, after, tiles, sem):
    del after
    slots = tiles.shape[0]
    n_live = live[0, 0]

    def tile_copy(slot):
        return pltpu.make_async_copy(cooccur.at[0, 0, slot], tiles.at[slot], sem.at[slot])

    for slot in range(slots):

        @pl.when(slot < n_live)
        def _():
            tile_copy(slot).start()

    for slot in range(slots):

        @pl.when(slot < n_live)
        def _():
            tile_copy(slot).wait()


def fetch(live, cooccur, after):
    _, _, slots, piece_rows, items = cooccur.shape
    return pl.pallas_call(
        fetch_kernel,
        out_shape=jax.ShapeDtypeStruct((slots, piece_rows, items), cooccur.dtype),
        in_specs=[
            pl.BlockSpec(memory_space=pltpu.SMEM),
            pl.BlockSpec(memory_space=pltpu.HBM),
            pl.BlockSpec(memory_space=pl.ANY),
        ],
        out_specs=pl.BlockSpec(memory_space=pltpu.VMEM),
        scratch_shapes=[pltpu.SemaphoreType.DMA((slots,))],
        compiler_params=pltpu.CompilerParams(vmem_limit_bytes=8 * MIB),
    )(live, cooccur, after)


def tile_kernel(distance, n_col, earlier, last, *refs):
    refs = list(refs)
    take = lambda count: [refs.pop(0) for _ in range(count)]
    live, pairs, tiles = take(3)
    row_refs = take(n_col)
    (window,) = take(1)
    prev = take(len(earlier))
    take(1)
    (right_out,) = take(1)
    left_outs = take(2 if last else 1)
    row_vecs, row_logs, right_acc = take(3)
    if last:
        left_acc, pieces = take(2)
    vec_sem, log_sem = take(2)
    if last:
        (piece_sem,) = take(1)
    slots, piece_rows, items = tiles.shape
    me = lax.axis_index("col")
    n_live = live[0, 0]
    scale = 1.0 / math.sqrt(items)

    def listed(slot):
        return jnp.logical_and(slot < n_live, pairs[0, 0, slot, 1] == distance)

    def row_copies(slot, source):
        first = pl.multiple_of(pairs[0, 0, slot, 2] * piece_rows, piece_rows)
        return (
            pltpu.make_async_copy(
                source.at[pl.ds(first, piece_rows)], row_vecs.at[slot], vec_sem.at[slot]
            ),
            pltpu.make_async_copy(
                source.at[pl.ds(items, LOG_ROWS)], row_logs.at[slot], log_sem.at[slot]
            ),
        )

    def piece_copy(slot, source):
        return pltpu.make_async_copy(source.at[slot], pieces.at[slot], piece_sem.at[slot])

    for slot in range(slots):

        @pl.when(listed(slot))
        def _():
            place = jnp.bitwise_xor(pairs[0, 0, slot, 0], me)
            for index in range(n_col):

                @pl.when(place == index)
                def _():
                    for copy in row_copies(slot, row_refs[index]):
                        copy.start()

        if last:
            for source, index in zip(prev, earlier):

                @pl.when(jnp.logical_and(slot < n_live, pairs[0, 0, slot, 1] == index))
                def _():
                    piece_copy(slot, source).start()

    any_listed = listed(0)
    for slot in range(1, slots):
        any_listed = jnp.logical_or(any_listed, listed(slot))

    @pl.when(any_listed)
    def _():
        right_acc[...] = jnp.zeros_like(right_acc)

    if last:
        left_acc[...] = jnp.zeros_like(left_acc)

    def add_left(slot, value):
        place = jnp.bitwise_xor(pairs[0, 0, slot, 0], me)
        first = place * items + pairs[0, 0, slot, 2] * piece_rows
        view = pl.ds(pl.multiple_of(first, piece_rows), piece_rows)
        left_acc[view, :] += value

    def one_tile(slot):
        for copy in row_copies(slot, row_refs[0]):
            copy.wait()
        piece = row_vecs[slot]
        piece_t = piece.T
        group = pairs[0, 0, slot, 2] * (piece_rows // LANES)
        logs = row_logs[slot]
        places = lax.broadcasted_iota(jnp.int32, (LOG_ROWS, LANES), 0)
        log_rows = []
        for part in range(piece_rows // LANES):
            chosen = jnp.where(places == group + part, 1.0, 0.0).astype(jnp.bfloat16)
            log_rows.append(
                lax.dot_general(
                    logs, chosen, (((0,), (0,)), ((), ())), preferred_element_type=jnp.float32
                )
            )
        row_term = jnp.concatenate(log_rows, axis=0) - LOG_SHIFT
        row_term = jnp.concatenate([row_term] * (CHUNK // LANES), axis=1)
        col_logs = window[items:, :].astype(jnp.float32)
        left = jnp.zeros((piece_rows, piece.shape[1]), jnp.float32)
        for chunk in range(items // CHUNK):
            cols = slice(chunk * CHUNK, (chunk + 1) * CHUNK)
            block = window[cols, :]
            per = CHUNK // LANES
            col_term = jnp.concatenate(
                [col_logs[chunk * per + i : chunk * per + i + 1] for i in range(per)], axis=1
            )
            scores = lax.dot_general(
                piece, block, (((1,), (1,)), ((), ())), preferred_element_type=jnp.float32
            )
            count = tiles[slot, :, cols].astype(jnp.float32)
            clipped = jnp.maximum(count, 1.0)
            misfit = (scores + row_term) + (col_term - jnp.log(clipped))
            root = clipped * lax.rsqrt(clipped)
            seen = (0.1 * scale + (0.25 * scale) * root) * misfit
            unseen = (0.5 * scale) * jnp.tanh(0.5 * misfit) + 0.5 * scale
            weights = jnp.where(count > 0, seen, unseen).astype(jnp.bfloat16)
            left = left + jnp.dot(weights, block, preferred_element_type=jnp.float32)
            right_acc[:, cols] += jnp.dot(piece_t, weights, preferred_element_type=jnp.float32)
        if last:
            add_left(slot, left)
        else:
            left_outs[0][slot] = left

    @pl.loop(0, slots)
    def _(slot):
        @pl.when(listed(slot))
        def _():
            one_tile(slot)

    @pl.when(any_listed)
    def _():
        right_out[...] = right_acc[...].T.astype(right_out.dtype)

    @pl.when(jnp.logical_not(any_listed))
    def _():
        right_out[...] = jnp.zeros_like(right_out)

    if last:

        @pl.loop(0, slots)
        def _(slot):
            @pl.when(jnp.logical_and(slot < n_live, jnp.logical_not(listed(slot))))
            def _():
                piece_copy(slot, prev[0]).wait()
                add_left(slot, pieces[slot])

        for index in range(n_col):
            block = left_acc[index * items : (index + 1) * items, :]
            if index % 2:
                left_outs[0][index // 2] = block.astype(jnp.bfloat16)
            else:
                left_outs[1][index // 2] = block


def run_tiles(distance, live, pairs, tiles, rows, window, earlier, last, dtype, after):
    slots, piece_rows, items = tiles.shape
    dim = window.shape[1]
    n_col = len(rows)
    any_spec = pl.BlockSpec(memory_space=pl.ANY)
    vmem_spec = pl.BlockSpec(memory_space=pltpu.VMEM)
    smem_spec = pl.BlockSpec(memory_space=pltpu.SMEM)
    right = jax.ShapeDtypeStruct((items, dim), dtype)
    scratch = [
        pltpu.VMEM((slots, piece_rows, dim), jnp.bfloat16),
        pltpu.VMEM((slots, LOG_ROWS, dim), jnp.bfloat16),
        pltpu.VMEM((dim, items), jnp.float32),
    ]
    sems = [pltpu.SemaphoreType.DMA((slots,))] * 2
    if last:
        outs = (
            right,
            jax.ShapeDtypeStruct((n_col // 2, items, dim), jnp.bfloat16),
            jax.ShapeDtypeStruct((n_col // 2, items, dim), jnp.float32),
        )
        scratch += [
            pltpu.VMEM((n_col * items, dim), jnp.float32),
            pltpu.VMEM((slots, piece_rows, dim), jnp.float32),
        ]
        sems += [pltpu.SemaphoreType.DMA((slots,))]
    else:
        outs = (right, jax.ShapeDtypeStruct((slots, piece_rows, dim), jnp.float32))
    return pl.pallas_call(
        functools.partial(tile_kernel, distance, n_col, tuple(earlier), last),
        out_shape=outs,
        in_specs=[smem_spec] * 2
        + [vmem_spec]
        + [any_spec] * n_col
        + [vmem_spec]
        + [any_spec] * (len(earlier) + 1),
        out_specs=tuple(vmem_spec for _ in outs),
        scratch_shapes=scratch + sems,
        compiler_params=pltpu.CompilerParams(vmem_limit_bytes=24 * MIB),
    )(live, pairs, tiles, *rows, window, *earlier.values(), after)


def shards(embedding, accumulator, popularity, cooccur, pair_list, live_count):
    items = embedding.shape[0]
    n_col = lax.axis_size("col")
    message = pack(embedding, popularity)
    reach = min(8, lax.axis_size("row"))
    windows = {0: message, 1: shifted(message, "row", -1)}
    if reach == 4:
        windows[3] = shifted(message, "row", -3)
        below = lax.ppermute(message, "row", [(3, 1)])
    rows = {0: message}
    bit = n_col // 2
    while bit:
        for place, block in list(rows.items()):
            if place:
                block, windows[1] = lax.optimization_barrier((block, windows[1]))
            rows[place ^ bit] = flipped(block, "col", bit)
        bit //= 2
    rows = [rows[place] for place in range(n_col)]
    if reach == 4:
        windows[2] = below + lax.ppermute(windows[1], "row", [(1, 0)])
    else:
        for distance in range(2, reach):
            windows[distance] = shifted(message, "row", -distance)
    tiles = fetch(live_count, cooccur, rows[1])
    right, earlier, received = {}, {}, {}
    order = [1, 0, *range(reach - 1, 1, -1)]
    for distance in order:
        last = distance == order[-1]
        done = run_tiles(
            distance,
            live_count,
            pair_list,
            tiles,
            rows,
            windows[distance],
            earlier,
            last,
            jnp.bfloat16 if distance else jnp.float32,
            received[1] if last else message,
        )
        right[distance], earlier[distance] = done[:2]
        if distance:
            received[distance] = shifted(right[distance], "row", distance)
    send, keep = done[1], done[2]
    keep = [keep[place] for place in range(n_col // 2)]
    ties = [received[distance] for distance in order[2:-1]]
    first, ties = lax.optimization_barrier((send[0], ties))
    got = [
        jnp.concatenate([flipped(part, "col", 1) for part in jnp.split(block, PARTS)])
        for block in [first, *[send[place] for place in range(1, n_col // 2)]]
    ]
    keep = [mine + got[place].astype(jnp.float32) for place, mine in enumerate(keep)]
    bit = 2
    while bit < n_col:
        sent = [keep[place].astype(jnp.bfloat16) for place in range(1, len(keep), 2)]
        keep = [
            keep[2 * place] + flipped(block, "col", bit).astype(jnp.float32)
            for place, block in enumerate(sent)
        ]
        bit *= 2
    gradient = right[0] + keep[0]
    for block in (received[1], *ties, received[order[-1]]):
        gradient = gradient + block.astype(jnp.float32)
    new_accumulator = accumulator + gradient * gradient
    new_embedding = embedding - LEARN_RATE * gradient / jnp.sqrt(new_accumulator)
    return (new_embedding, new_accumulator)


def solution(mesh):
    in_specs = (
        P(("parts", "row", "col"), None),
        P(("parts", "row", "col"), None),
        P(("parts", "row", "col")),
        P(("parts", "row"), "col", None, None, None),
        P(("parts", "row"), "col", None, None),
        P(("parts", "row"), "col"),
    )
    out_specs = (P(("parts", "row", "col"), None), P(("parts", "row", "col"), None))
    return jax.shard_map(shards, mesh=mesh, in_specs=in_specs, out_specs=out_specs, check_vma=False)
```

```python
import functools
import math

import jax
import jax.numpy as jnp
from jax import lax
from jax.experimental import pallas as pl
from jax.experimental.pallas import tpu as pltpu
from jax.sharding import PartitionSpec as P

LOG_SHIFT = 4.0
LEARN_RATE = 0.5
LANES = 128
LOG_ROWS = 16
CHUNK = 1024
MIB = 1 << 20
PARTS = 2


def shifted(array, axis, by):
    count = lax.axis_size(axis)
    pairs = [(i, i + by) for i in range(count) if 0 <= i + by < count]
    return lax.ppermute(array, axis, pairs)


def flipped(array, axis, bit):
    count = lax.axis_size(axis)
    return lax.ppermute(array, axis, [(i, i ^ bit) for i in range(count)])


def pack_kernel(embedding, popularity, message):
    items = embedding.shape[0]
    message[:items] = embedding[...].astype(jnp.bfloat16)
    logs = jnp.log(popularity[...].astype(jnp.float32))
    message[items:] = jnp.concatenate([logs, jnp.zeros_like(logs)], axis=0).astype(jnp.bfloat16)


def pack(embedding, popularity):
    items, dim = embedding.shape
    return pl.pallas_call(
        pack_kernel,
        out_shape=jax.ShapeDtypeStruct((items + LOG_ROWS, dim), jnp.bfloat16),
        in_specs=[pl.BlockSpec(memory_space=pltpu.VMEM)] * 2,
        out_specs=pl.BlockSpec(memory_space=pltpu.VMEM),
        compiler_params=pltpu.CompilerParams(vmem_limit_bytes=4 * MIB),
    )(embedding, popularity.reshape(items // LANES, LANES))


def fetch_kernel(live, pairs, cooccur, tiles, sem):
    del pairs
    slots = tiles.shape[0]
    n_live = live[0, 0]

    def tile_copy(slot):
        return pltpu.make_async_copy(cooccur.at[0, 0, slot], tiles.at[slot], sem.at[slot])

    for slot in range(slots):

        @pl.when(slot < n_live)
        def _():
            tile_copy(slot).start()

    for slot in range(slots):

        @pl.when(slot < n_live)
        def _():
            tile_copy(slot).wait()


def fetch(live, pairs, cooccur):
    _, _, slots, piece_rows, items = cooccur.shape
    return pl.pallas_call(
        fetch_kernel,
        out_shape=jax.ShapeDtypeStruct((slots, piece_rows, items), cooccur.dtype),
        in_specs=[
            pl.BlockSpec(memory_space=pltpu.SMEM),
            pl.BlockSpec(memory_space=pltpu.SMEM),
            pl.BlockSpec(memory_space=pltpu.HBM),
        ],
        out_specs=pl.BlockSpec(memory_space=pltpu.VMEM),
        scratch_shapes=[pltpu.SemaphoreType.DMA((slots,))],
        compiler_params=pltpu.CompilerParams(vmem_limit_bytes=8 * MIB),
    )(live, pairs, cooccur)


def tile_kernel(distance, n_col, earlier, last, *refs):
    refs = list(refs)
    take = lambda count: [refs.pop(0) for _ in range(count)]
    live, pairs, tiles = take(3)
    row_refs = take(n_col)
    (window,) = take(1)
    prev = take(len(earlier))
    take(1)
    (right_out,) = take(1)
    left_outs = take(2 if last else 1)
    row_vecs, row_logs, right_acc = take(3)
    if last:
        left_acc, pieces = take(2)
    vec_sem, log_sem = take(2)
    if last:
        (piece_sem,) = take(1)
    slots, piece_rows, items = tiles.shape
    me = lax.axis_index("col")
    n_live = live[0, 0]
    scale = 1.0 / math.sqrt(items)

    def listed(slot):
        return jnp.logical_and(slot < n_live, pairs[0, 0, slot, 1] == distance)

    def row_copies(slot, source):
        first = pl.multiple_of(pairs[0, 0, slot, 2] * piece_rows, piece_rows)
        return (
            pltpu.make_async_copy(
                source.at[pl.ds(first, piece_rows)], row_vecs.at[slot], vec_sem.at[slot]
            ),
            pltpu.make_async_copy(
                source.at[pl.ds(items, LOG_ROWS)], row_logs.at[slot], log_sem.at[slot]
            ),
        )

    def piece_copy(slot, source):
        return pltpu.make_async_copy(source.at[slot], pieces.at[slot], piece_sem.at[slot])

    for slot in range(slots):

        @pl.when(listed(slot))
        def _():
            place = jnp.bitwise_xor(pairs[0, 0, slot, 0], me)
            for index in range(n_col):

                @pl.when(place == index)
                def _():
                    for copy in row_copies(slot, row_refs[index]):
                        copy.start()

        if last:
            for source, index in zip(prev, earlier):

                @pl.when(jnp.logical_and(slot < n_live, pairs[0, 0, slot, 1] == index))
                def _():
                    piece_copy(slot, source).start()

    any_listed = listed(0)
    for slot in range(1, slots):
        any_listed = jnp.logical_or(any_listed, listed(slot))

    @pl.when(any_listed)
    def _():
        right_acc[...] = jnp.zeros_like(right_acc)

    if last:
        left_acc[...] = jnp.zeros_like(left_acc)

    def add_left(slot, value):
        place = jnp.bitwise_xor(pairs[0, 0, slot, 0], me)
        first = place * items + pairs[0, 0, slot, 2] * piece_rows
        view = pl.ds(pl.multiple_of(first, piece_rows), piece_rows)
        left_acc[view, :] += value

    def one_tile(slot):
        for copy in row_copies(slot, row_refs[0]):
            copy.wait()
        piece = row_vecs[slot]
        piece_t = piece.T
        group = pairs[0, 0, slot, 2] * (piece_rows // LANES)
        logs = row_logs[slot]
        places = lax.broadcasted_iota(jnp.int32, (LOG_ROWS, LANES), 0)
        log_rows = []
        for part in range(piece_rows // LANES):
            chosen = jnp.where(places == group + part, 1.0, 0.0).astype(jnp.bfloat16)
            log_rows.append(
                lax.dot_general(
                    logs, chosen, (((0,), (0,)), ((), ())), preferred_element_type=jnp.float32
                )
            )
        row_term = jnp.concatenate(log_rows, axis=0) - LOG_SHIFT
        row_term = jnp.concatenate([row_term] * (CHUNK // LANES), axis=1)
        col_logs = window[items:, :].astype(jnp.float32)
        left = jnp.zeros((piece_rows, piece.shape[1]), jnp.float32)
        for chunk in range(items // CHUNK):
            cols = slice(chunk * CHUNK, (chunk + 1) * CHUNK)
            block = window[cols, :]
            per = CHUNK // LANES
            col_term = jnp.concatenate(
                [col_logs[chunk * per + i : chunk * per + i + 1] for i in range(per)], axis=1
            )
            scores = lax.dot_general(
                piece, block, (((1,), (1,)), ((), ())), preferred_element_type=jnp.float32
            )
            count = tiles[slot, :, cols].astype(jnp.float32)
            clipped = jnp.maximum(count, 1.0)
            misfit = (scores + row_term) + (col_term - jnp.log(clipped))
            root = clipped * lax.rsqrt(clipped)
            seen = (0.1 * scale + (0.25 * scale) * root) * misfit
            unseen = (0.5 * scale) * jnp.tanh(0.5 * misfit) + 0.5 * scale
            weights = jnp.where(count > 0, seen, unseen).astype(jnp.bfloat16)
            left = left + jnp.dot(weights, block, preferred_element_type=jnp.float32)
            right_acc[:, cols] += jnp.dot(piece_t, weights, preferred_element_type=jnp.float32)
        if last:
            add_left(slot, left)
        else:
            left_outs[0][slot] = left

    @pl.loop(0, slots)
    def _(slot):
        @pl.when(listed(slot))
        def _():
            one_tile(slot)

    @pl.when(any_listed)
    def _():
        right_out[...] = right_acc[...].T.astype(right_out.dtype)

    @pl.when(jnp.logical_not(any_listed))
    def _():
        right_out[...] = jnp.zeros_like(right_out)

    if last:

        @pl.loop(0, slots)
        def _(slot):
            @pl.when(jnp.logical_and(slot < n_live, jnp.logical_not(listed(slot))))
            def _():
                piece_copy(slot, prev[0]).wait()
                add_left(slot, pieces[slot])

        for index in range(n_col):
            block = left_acc[index * items : (index + 1) * items, :]
            if index % 2:
                left_outs[0][index // 2] = block.astype(jnp.bfloat16)
            else:
                left_outs[1][index // 2] = block


def run_tiles(distance, live, pairs, tiles, rows, window, earlier, last, dtype, after):
    slots, piece_rows, items = tiles.shape
    dim = window.shape[1]
    n_col = len(rows)
    any_spec = pl.BlockSpec(memory_space=pl.ANY)
    vmem_spec = pl.BlockSpec(memory_space=pltpu.VMEM)
    smem_spec = pl.BlockSpec(memory_space=pltpu.SMEM)
    right = jax.ShapeDtypeStruct((items, dim), dtype)
    scratch = [
        pltpu.VMEM((slots, piece_rows, dim), jnp.bfloat16),
        pltpu.VMEM((slots, LOG_ROWS, dim), jnp.bfloat16),
        pltpu.VMEM((dim, items), jnp.float32),
    ]
    sems = [pltpu.SemaphoreType.DMA((slots,))] * 2
    if last:
        outs = (
            right,
            jax.ShapeDtypeStruct((n_col // 2, items, dim), jnp.bfloat16),
            jax.ShapeDtypeStruct((n_col // 2, items, dim), jnp.float32),
        )
        scratch += [
            pltpu.VMEM((n_col * items, dim), jnp.float32),
            pltpu.VMEM((slots, piece_rows, dim), jnp.float32),
        ]
        sems += [pltpu.SemaphoreType.DMA((slots,))]
    else:
        outs = (right, jax.ShapeDtypeStruct((slots, piece_rows, dim), jnp.float32))
    return pl.pallas_call(
        functools.partial(tile_kernel, distance, n_col, tuple(earlier), last),
        out_shape=outs,
        in_specs=[smem_spec] * 2
        + [vmem_spec]
        + [any_spec] * n_col
        + [vmem_spec]
        + [any_spec] * (len(earlier) + 1),
        out_specs=tuple(vmem_spec for _ in outs),
        scratch_shapes=scratch + sems,
        compiler_params=pltpu.CompilerParams(vmem_limit_bytes=24 * MIB),
    )(live, pairs, tiles, *rows, window, *earlier.values(), after)


def shards(embedding, accumulator, popularity, cooccur, pair_list, live_count):
    items = embedding.shape[0]
    n_col = lax.axis_size("col")
    message = pack(embedding, popularity)
    reach = min(8, lax.axis_size("row"))
    windows = {0: message, 1: shifted(message, "row", -1)}
    if reach == 4:
        windows[3] = shifted(message, "row", -3)
        below = lax.ppermute(message, "row", [(3, 1)])
    tiles = fetch(live_count, pair_list, cooccur)
    rows = {0: message}
    bit = n_col // 2
    while bit:
        for place, block in list(rows.items()):
            if place:
                block, windows[1], tiles = lax.optimization_barrier((block, windows[1], tiles))
                rows[place ^ bit] = flipped(block, "col", bit)
            else:
                rows[place ^ bit] = flipped(block, "col", bit)
        bit //= 2
    rows = [rows[place] for place in range(n_col)]
    if reach == 4:
        windows[2] = below + lax.ppermute(windows[1], "row", [(1, 0)])
    else:
        for distance in range(2, reach):
            windows[distance] = shifted(message, "row", -distance)
    right, earlier, received = {}, {}, {}
    order = [1, 0, *range(reach - 1, 1, -1)]
    for distance in order:
        last = distance == order[-1]
        done = run_tiles(
            distance,
            live_count,
            pair_list,
            tiles,
            rows,
            windows[distance],
            earlier,
            last,
            jnp.bfloat16 if distance else jnp.float32,
            received[1] if last else message,
        )
        right[distance], earlier[distance] = done[:2]
        if distance:
            received[distance] = shifted(right[distance], "row", distance)
    send, keep = done[1], done[2]
    keep = [keep[place] for place in range(n_col // 2)]
    ties = [received[distance] for distance in order[2:-1]]
    first, ties = lax.optimization_barrier((send[0], ties))
    got = [
        jnp.concatenate([flipped(part, "col", 1) for part in jnp.split(block, PARTS)])
        for block in [first, *[send[place] for place in range(1, n_col // 2)]]
    ]
    keep = [mine + got[place].astype(jnp.float32) for place, mine in enumerate(keep)]
    bit = 2
    while bit < n_col:
        sent = [keep[place].astype(jnp.bfloat16) for place in range(1, len(keep), 2)]
        keep = [
            keep[2 * place] + flipped(block, "col", bit).astype(jnp.float32)
            for place, block in enumerate(sent)
        ]
        bit *= 2
    gradient = right[0] + keep[0]
    for block in (received[1], *ties, received[order[-1]]):
        gradient = gradient + block.astype(jnp.float32)
    new_accumulator = accumulator + gradient * gradient
    new_embedding = embedding - LEARN_RATE * gradient / jnp.sqrt(new_accumulator)
    return (new_embedding, new_accumulator)


def solution(mesh):
    in_specs = (
        P(("parts", "row", "col"), None),
        P(("parts", "row", "col"), None),
        P(("parts", "row", "col")),
        P(("parts", "row"), "col", None, None, None),
        P(("parts", "row"), "col", None, None),
        P(("parts", "row"), "col"),
    )
    out_specs = (P(("parts", "row", "col"), None), P(("parts", "row", "col"), None))
    return jax.shard_map(shards, mesh=mesh, in_specs=in_specs, out_specs=out_specs, check_vma=False)
```

```python
import functools
import math

import jax
import jax.numpy as jnp
from jax import lax
from jax.experimental import pallas as pl
from jax.experimental.pallas import tpu as pltpu
from jax.sharding import PartitionSpec as P

LOG_SHIFT = 4.0
LEARN_RATE = 0.5
LANES = 128
LOG_ROWS = 16
CHUNK = 1024
STRIP = 32
MIB = 1 << 20
PARTS = 2


def shifted(array, axis, by):
    count = lax.axis_size(axis)
    pairs = [(i, i + by) for i in range(count) if 0 <= i + by < count]
    return lax.ppermute(array, axis, pairs)


def flipped(array, axis, bit):
    count = lax.axis_size(axis)
    return lax.ppermute(array, axis, [(i, i ^ bit) for i in range(count)])


def pack_kernel(embedding, popularity, message):
    items = embedding.shape[0]
    message[:items] = embedding[...].astype(jnp.bfloat16)
    logs = jnp.log(popularity[...].astype(jnp.float32))
    message[items:] = jnp.concatenate([logs, jnp.zeros_like(logs)], axis=0).astype(jnp.bfloat16)


def pack(embedding, popularity):
    items, dim = embedding.shape
    return pl.pallas_call(
        pack_kernel,
        out_shape=jax.ShapeDtypeStruct((items + LOG_ROWS, dim), jnp.bfloat16),
        in_specs=[pl.BlockSpec(memory_space=pltpu.VMEM)] * 2,
        out_specs=pl.BlockSpec(memory_space=pltpu.VMEM),
        compiler_params=pltpu.CompilerParams(vmem_limit_bytes=4 * MIB),
    )(embedding, popularity.reshape(items // LANES, LANES))


def fetch_kernel(listing, cooccur, gains, targets):
    slots, piece_rows, items = gains.shape
    scale = 1.0 / math.sqrt(items)
    n_live = listing[0, 3 * slots]

    @pl.loop(0, slots)
    def _(slot):
        @pl.when(slot < n_live)
        def _():
            @pl.loop(0, piece_rows // STRIP)
            def _(strip):
                rows = pl.ds(pl.multiple_of(strip * STRIP, STRIP), STRIP)
                count = cooccur[0, 0, slot, rows, :].astype(jnp.float32)
                clipped = jnp.maximum(count, 1.0)
                root = clipped * lax.rsqrt(clipped)
                gain = 0.1 * scale + (0.25 * scale) * root
                gains[slot, rows, :] = jnp.where(count > 0, gain, 0.0)
                targets[slot, rows, :] = jnp.log(clipped)


def fetch(listing, cooccur):
    _, _, slots, piece_rows, items = cooccur.shape
    shape = jax.ShapeDtypeStruct((slots, piece_rows, items), jnp.float32)
    vmem_spec = pl.BlockSpec(memory_space=pltpu.VMEM)
    return pl.pallas_call(
        fetch_kernel,
        out_shape=(shape, shape),
        in_specs=[vmem_spec, vmem_spec],
        out_specs=(vmem_spec, vmem_spec),
        compiler_params=pltpu.CompilerParams(vmem_limit_bytes=24 * MIB),
    )(listing, cooccur)


def tile_kernel(distance, n_col, earlier, last, *refs):
    refs = list(refs)
    take = lambda count: [refs.pop(0) for _ in range(count)]
    listing, gains, targets = take(3)
    row_refs = take(n_col)
    (window,) = take(1)
    prev = take(len(earlier))
    take(1)
    (right_out,) = take(1)
    left_outs = take(2 if last else 1)
    pairs, row_vecs, row_logs, right_acc = take(4)
    if last:
        left_acc, pieces = take(2)
    vec_sem, log_sem = take(2)
    if last:
        (piece_sem,) = take(1)
    slots, piece_rows, items = gains.shape
    me = lax.axis_index("col")
    n_live = listing[0, 3 * slots]
    for index in range(3 * slots):
        pairs[index] = listing[0, index]
    scale = 1.0 / math.sqrt(items)

    def listed(slot):
        return jnp.logical_and(slot < n_live, pairs[slots + slot] == distance)

    def row_copies(slot, source):
        first = pl.multiple_of(pairs[2 * slots + slot] * piece_rows, piece_rows)
        return (
            pltpu.make_async_copy(
                source.at[pl.ds(first, piece_rows)], row_vecs.at[slot], vec_sem.at[slot]
            ),
            pltpu.make_async_copy(
                source.at[pl.ds(items, LOG_ROWS)], row_logs.at[slot], log_sem.at[slot]
            ),
        )

    def piece_copy(slot, source):
        return pltpu.make_async_copy(source.at[slot], pieces.at[slot], piece_sem.at[slot])

    for slot in range(slots):

        @pl.when(listed(slot))
        def _():
            place = jnp.bitwise_xor(pairs[slot], me)
            for index in range(n_col):

                @pl.when(place == index)
                def _():
                    for copy in row_copies(slot, row_refs[index]):
                        copy.start()

        if last:
            for source, index in zip(prev, earlier):

                @pl.when(jnp.logical_and(slot < n_live, pairs[slots + slot] == index))
                def _():
                    piece_copy(slot, source).start()

    any_listed = listed(0)
    for slot in range(1, slots):
        any_listed = jnp.logical_or(any_listed, listed(slot))

    @pl.when(any_listed)
    def _():
        right_acc[...] = jnp.zeros_like(right_acc)

    if last:
        left_acc[...] = jnp.zeros_like(left_acc)

    def add_left(slot, value):
        place = jnp.bitwise_xor(pairs[slot], me)
        first = place * items + pairs[2 * slots + slot] * piece_rows
        view = pl.ds(pl.multiple_of(first, piece_rows), piece_rows)
        left_acc[view, :] += value

    def one_tile(slot):
        for copy in row_copies(slot, row_refs[0]):
            copy.wait()
        piece = row_vecs[slot]
        piece_t = piece.T
        group = pairs[2 * slots + slot] * (piece_rows // LANES)
        logs = row_logs[slot]
        places = lax.broadcasted_iota(jnp.int32, (LOG_ROWS, LANES), 0)
        log_rows = []
        for part in range(piece_rows // LANES):
            chosen = jnp.where(places == group + part, 1.0, 0.0).astype(jnp.bfloat16)
            log_rows.append(
                lax.dot_general(
                    logs, chosen, (((0,), (0,)), ((), ())), preferred_element_type=jnp.float32
                )
            )
        row_term = jnp.concatenate(log_rows, axis=0) - LOG_SHIFT
        row_term = jnp.concatenate([row_term] * (CHUNK // LANES), axis=1)
        col_logs = window[items:, :].astype(jnp.float32)
        left = jnp.zeros((piece_rows, piece.shape[1]), jnp.float32)
        for chunk in range(items // CHUNK):
            cols = slice(chunk * CHUNK, (chunk + 1) * CHUNK)
            block = window[cols, :]
            per = CHUNK // LANES
            col_term = jnp.concatenate(
                [col_logs[chunk * per + i : chunk * per + i + 1] for i in range(per)], axis=1
            )
            scores = lax.dot_general(
                piece, block, (((1,), (1,)), ((), ())), preferred_element_type=jnp.float32
            )
            gain = gains[slot, :, cols]
            misfit = (scores + row_term) + (col_term - targets[slot, :, cols])
            unseen = (0.5 * scale) * jnp.tanh(0.5 * misfit) + 0.5 * scale
            weights = jnp.where(gain > 0, gain * misfit, unseen).astype(jnp.bfloat16)
            left = left + jnp.dot(weights, block, preferred_element_type=jnp.float32)
            right_acc[:, cols] += jnp.dot(piece_t, weights, preferred_element_type=jnp.float32)
        if last:
            add_left(slot, left)
        else:
            left_outs[0][slot] = left

    @pl.loop(0, slots)
    def _(slot):
        @pl.when(listed(slot))
        def _():
            one_tile(slot)

    @pl.when(any_listed)
    def _():
        right_out[...] = right_acc[...].T.astype(right_out.dtype)

    @pl.when(jnp.logical_not(any_listed))
    def _():
        right_out[...] = jnp.zeros_like(right_out)

    if last:

        @pl.loop(0, slots)
        def _(slot):
            @pl.when(jnp.logical_and(slot < n_live, jnp.logical_not(listed(slot))))
            def _():
                piece_copy(slot, prev[0]).wait()
                add_left(slot, pieces[slot])

        for index in range(n_col):
            block = left_acc[index * items : (index + 1) * items, :]
            if index % 2:
                left_outs[0][index // 2] = block.astype(jnp.bfloat16)
            else:
                left_outs[1][index // 2] = block


def run_tiles(distance, listing, tiles, rows, window, earlier, last, dtype, after):
    slots, piece_rows, items = tiles[0].shape
    dim = window.shape[1]
    n_col = len(rows)
    any_spec = pl.BlockSpec(memory_space=pl.ANY)
    vmem_spec = pl.BlockSpec(memory_space=pltpu.VMEM)
    right = jax.ShapeDtypeStruct((items, dim), dtype)
    scratch = [
        pltpu.SMEM((3 * slots,), jnp.int32),
        pltpu.VMEM((slots, piece_rows, dim), jnp.bfloat16),
        pltpu.VMEM((slots, LOG_ROWS, dim), jnp.bfloat16),
        pltpu.VMEM((dim, items), jnp.float32),
    ]
    sems = [pltpu.SemaphoreType.DMA((slots,))] * 2
    if last:
        outs = (
            right,
            jax.ShapeDtypeStruct((n_col // 2, items, dim), jnp.bfloat16),
            jax.ShapeDtypeStruct((n_col // 2, items, dim), jnp.float32),
        )
        scratch += [
            pltpu.VMEM((n_col * items, dim), jnp.float32),
            pltpu.VMEM((slots, piece_rows, dim), jnp.float32),
        ]
        sems += [pltpu.SemaphoreType.DMA((slots,))]
    else:
        outs = (right, jax.ShapeDtypeStruct((slots, piece_rows, dim), jnp.float32))
    return pl.pallas_call(
        functools.partial(tile_kernel, distance, n_col, tuple(earlier), last),
        out_shape=outs,
        in_specs=[vmem_spec] * 3
        + [any_spec] * n_col
        + [vmem_spec]
        + [any_spec] * (len(earlier) + 1),
        out_specs=tuple(vmem_spec for _ in outs),
        scratch_shapes=scratch + sems,
        compiler_params=pltpu.CompilerParams(vmem_limit_bytes=24 * MIB),
    )(listing, *tiles, *rows, window, *earlier.values(), after)


def shards(embedding, accumulator, popularity, cooccur, pair_list, live_count):
    items = embedding.shape[0]
    n_col = lax.axis_size("col")
    listing = jnp.transpose(pair_list, (0, 3, 1, 2)).reshape(1, -1)
    listing = jnp.concatenate([listing, live_count], axis=1)
    listing = jnp.pad(listing, ((0, 7), (0, LANES - listing.shape[1])))
    message = pack(embedding, popularity)
    reach = min(8, lax.axis_size("row"))
    windows = {0: message, 1: shifted(message, "row", -1)}
    if reach == 4:
        windows[3] = shifted(message, "row", -3)
        below = lax.ppermute(message, "row", [(3, 1)])
    tiles = fetch(listing, cooccur)
    rows = {0: message}
    bit = n_col // 2
    while bit:
        for place, block in list(rows.items()):
            if place:
                block, windows[1], tiles = lax.optimization_barrier((block, windows[1], tiles))
                rows[place ^ bit] = flipped(block, "col", bit)
            else:
                rows[place ^ bit] = flipped(block, "col", bit)
        bit //= 2
    rows = [rows[place] for place in range(n_col)]
    if reach == 4:
        windows[2] = below + lax.ppermute(windows[1], "row", [(1, 0)])
    else:
        for distance in range(2, reach):
            windows[distance] = shifted(message, "row", -distance)
    right, earlier, received = {}, {}, {}
    order = [1, 0, *range(reach - 1, 1, -1)]
    for distance in order:
        last = distance == order[-1]
        done = run_tiles(
            distance,
            listing,
            tiles,
            rows,
            windows[distance],
            earlier,
            last,
            jnp.bfloat16 if distance else jnp.float32,
            received[1] if last else message,
        )
        right[distance], earlier[distance] = done[:2]
        if distance:
            received[distance] = shifted(right[distance], "row", distance)
    send, keep = done[1], done[2]
    keep = [keep[place] for place in range(n_col // 2)]
    ties = [received[distance] for distance in order[2:-1]]
    first, ties = lax.optimization_barrier((send[0], ties))
    got = [
        jnp.concatenate([flipped(part, "col", 1) for part in jnp.split(block, PARTS)])
        for block in [first, *[send[place] for place in range(1, n_col // 2)]]
    ]
    keep = [mine + got[place].astype(jnp.float32) for place, mine in enumerate(keep)]
    bit = 2
    while bit < n_col:
        sent = [keep[place].astype(jnp.bfloat16) for place in range(1, len(keep), 2)]
        keep = [
            keep[2 * place] + flipped(block, "col", bit).astype(jnp.float32)
            for place, block in enumerate(sent)
        ]
        bit *= 2
    gradient = right[0] + keep[0]
    for block in (received[1], *ties, received[order[-1]]):
        gradient = gradient + block.astype(jnp.float32)
    new_accumulator = accumulator + gradient * gradient
    new_embedding = embedding - LEARN_RATE * gradient / jnp.sqrt(new_accumulator)
    return (new_embedding, new_accumulator)


def solution(mesh):
    in_specs = (
        P(("parts", "row", "col"), None),
        P(("parts", "row", "col"), None),
        P(("parts", "row", "col")),
        P(("parts", "row"), "col", None, None, None),
        P(("parts", "row"), "col", None, None),
        P(("parts", "row"), "col"),
    )
    out_specs = (P(("parts", "row", "col"), None), P(("parts", "row", "col"), None))
    return jax.shard_map(shards, mesh=mesh, in_specs=in_specs, out_specs=out_specs, check_vma=False)
```

```python
import functools
import math

import jax
import jax.numpy as jnp
from jax import lax
from jax.experimental import pallas as pl
from jax.experimental.pallas import tpu as pltpu
from jax.sharding import PartitionSpec as P

LOG_SHIFT = 4.0
LEARN_RATE = 0.5
LANES = 128
LOG_ROWS = 16
CHUNK = 1024
STRIP = 32
MIB = 1 << 20
PARTS = 1


def shifted(array, axis, by):
    count = lax.axis_size(axis)
    pairs = [(i, i + by) for i in range(count) if 0 <= i + by < count]
    return lax.ppermute(array, axis, pairs)


def flipped(array, axis, bit):
    count = lax.axis_size(axis)
    return lax.ppermute(array, axis, [(i, i ^ bit) for i in range(count)])


def pack_kernel(embedding, popularity, message):
    items = embedding.shape[0]
    message[:items] = embedding[...].astype(jnp.bfloat16)
    logs = jnp.log(popularity[...].astype(jnp.float32))
    message[items:] = jnp.concatenate([logs, jnp.zeros_like(logs)], axis=0).astype(jnp.bfloat16)


def pack(embedding, popularity):
    items, dim = embedding.shape
    return pl.pallas_call(
        pack_kernel,
        out_shape=jax.ShapeDtypeStruct((items + LOG_ROWS, dim), jnp.bfloat16),
        in_specs=[pl.BlockSpec(memory_space=pltpu.VMEM)] * 2,
        out_specs=pl.BlockSpec(memory_space=pltpu.VMEM),
        compiler_params=pltpu.CompilerParams(vmem_limit_bytes=4 * MIB),
    )(embedding, popularity.reshape(items // LANES, LANES))


def fetch_kernel(listing, cooccur, gains, targets):
    slots, piece_rows, items = gains.shape
    scale = 1.0 / math.sqrt(items)
    n_live = listing[0, 3 * slots]

    @pl.loop(0, slots)
    def _(slot):
        @pl.when(slot < n_live)
        def _():
            @pl.loop(0, piece_rows // STRIP)
            def _(strip):
                rows = pl.ds(pl.multiple_of(strip * STRIP, STRIP), STRIP)
                count = cooccur[0, 0, slot, rows, :].astype(jnp.float32)
                clipped = jnp.maximum(count, 1.0)
                root = clipped * lax.rsqrt(clipped)
                gain = 0.1 * scale + (0.25 * scale) * root
                gains[slot, rows, :] = jnp.where(count > 0, gain, 0.0)
                targets[slot, rows, :] = jnp.log(clipped)


def fetch(listing, cooccur):
    _, _, slots, piece_rows, items = cooccur.shape
    shape = jax.ShapeDtypeStruct((slots, piece_rows, items), jnp.float32)
    vmem_spec = pl.BlockSpec(memory_space=pltpu.VMEM)
    return pl.pallas_call(
        fetch_kernel,
        out_shape=(shape, shape),
        in_specs=[vmem_spec, vmem_spec],
        out_specs=(vmem_spec, vmem_spec),
        compiler_params=pltpu.CompilerParams(vmem_limit_bytes=24 * MIB),
    )(listing, cooccur)


def tile_kernel(distance, n_col, earlier, last, *refs):
    refs = list(refs)
    take = lambda count: [refs.pop(0) for _ in range(count)]
    listing, gains, targets = take(3)
    row_refs = take(n_col)
    (window,) = take(1)
    prev = take(len(earlier))
    take(1)
    (right_out,) = take(1)
    left_outs = take(2 if last else 1)
    pairs, row_vecs, row_logs, right_acc = take(4)
    if last:
        left_acc, pieces = take(2)
    vec_sem, log_sem = take(2)
    if last:
        (piece_sem,) = take(1)
    slots, piece_rows, items = gains.shape
    me = lax.axis_index("col")
    n_live = listing[0, 3 * slots]
    for index in range(3 * slots):
        pairs[index] = listing[0, index]
    scale = 1.0 / math.sqrt(items)

    def listed(slot):
        return jnp.logical_and(slot < n_live, pairs[slots + slot] == distance)

    def row_copies(slot, source):
        first = pl.multiple_of(pairs[2 * slots + slot] * piece_rows, piece_rows)
        return (
            pltpu.make_async_copy(
                source.at[pl.ds(first, piece_rows)], row_vecs.at[slot], vec_sem.at[slot]
            ),
            pltpu.make_async_copy(
                source.at[pl.ds(items, LOG_ROWS)], row_logs.at[slot], log_sem.at[slot]
            ),
        )

    def piece_copy(slot, source):
        return pltpu.make_async_copy(source.at[slot], pieces.at[slot], piece_sem.at[slot])

    for slot in range(slots):

        @pl.when(listed(slot))
        def _():
            place = jnp.bitwise_xor(pairs[slot], me)
            for index in range(n_col):

                @pl.when(place == index)
                def _():
                    for copy in row_copies(slot, row_refs[index]):
                        copy.start()

        if last:
            for source, index in zip(prev, earlier):

                @pl.when(jnp.logical_and(slot < n_live, pairs[slots + slot] == index))
                def _():
                    piece_copy(slot, source).start()

    any_listed = listed(0)
    for slot in range(1, slots):
        any_listed = jnp.logical_or(any_listed, listed(slot))

    @pl.when(any_listed)
    def _():
        right_acc[...] = jnp.zeros_like(right_acc)

    if last:
        left_acc[...] = jnp.zeros_like(left_acc)

    def add_left(slot, value):
        place = jnp.bitwise_xor(pairs[slot], me)
        first = place * items + pairs[2 * slots + slot] * piece_rows
        view = pl.ds(pl.multiple_of(first, piece_rows), piece_rows)
        left_acc[view, :] += value

    def one_tile(slot):
        for copy in row_copies(slot, row_refs[0]):
            copy.wait()
        piece = row_vecs[slot]
        piece_t = piece.T
        group = pairs[2 * slots + slot] * (piece_rows // LANES)
        logs = row_logs[slot]
        places = lax.broadcasted_iota(jnp.int32, (LOG_ROWS, LANES), 0)
        log_rows = []
        for part in range(piece_rows // LANES):
            chosen = jnp.where(places == group + part, 1.0, 0.0).astype(jnp.bfloat16)
            log_rows.append(
                lax.dot_general(
                    logs, chosen, (((0,), (0,)), ((), ())), preferred_element_type=jnp.float32
                )
            )
        row_term = jnp.concatenate(log_rows, axis=0) - LOG_SHIFT
        row_term = jnp.concatenate([row_term] * (CHUNK // LANES), axis=1)
        col_logs = window[items:, :].astype(jnp.float32)
        left = jnp.zeros((piece_rows, piece.shape[1]), jnp.float32)
        for chunk in range(items // CHUNK):
            cols = slice(chunk * CHUNK, (chunk + 1) * CHUNK)
            block = window[cols, :]
            per = CHUNK // LANES
            col_term = jnp.concatenate(
                [col_logs[chunk * per + i : chunk * per + i + 1] for i in range(per)], axis=1
            )
            scores = lax.dot_general(
                piece, block, (((1,), (1,)), ((), ())), preferred_element_type=jnp.float32
            )
            gain = gains[slot, :, cols]
            misfit = (scores + row_term) + (col_term - targets[slot, :, cols])
            unseen = (0.5 * scale) * jnp.tanh(0.5 * misfit) + 0.5 * scale
            weights = jnp.where(gain > 0, gain * misfit, unseen).astype(jnp.bfloat16)
            left = left + jnp.dot(weights, block, preferred_element_type=jnp.float32)
            right_acc[:, cols] += jnp.dot(piece_t, weights, preferred_element_type=jnp.float32)
        if last:
            add_left(slot, left)
        else:
            left_outs[0][slot] = left

    @pl.loop(0, slots)
    def _(slot):
        @pl.when(listed(slot))
        def _():
            one_tile(slot)

    @pl.when(any_listed)
    def _():
        right_out[...] = right_acc[...].T.astype(right_out.dtype)

    @pl.when(jnp.logical_not(any_listed))
    def _():
        right_out[...] = jnp.zeros_like(right_out)

    if last:

        @pl.loop(0, slots)
        def _(slot):
            @pl.when(jnp.logical_and(slot < n_live, jnp.logical_not(listed(slot))))
            def _():
                piece_copy(slot, prev[0]).wait()
                add_left(slot, pieces[slot])

        for index in range(n_col):
            block = left_acc[index * items : (index + 1) * items, :]
            if index % 2:
                left_outs[0][index // 2] = block.astype(jnp.bfloat16)
            else:
                left_outs[1][index // 2] = block


def run_tiles(distance, listing, tiles, rows, window, earlier, last, dtype, after):
    slots, piece_rows, items = tiles[0].shape
    dim = window.shape[1]
    n_col = len(rows)
    any_spec = pl.BlockSpec(memory_space=pl.ANY)
    vmem_spec = pl.BlockSpec(memory_space=pltpu.VMEM)
    right = jax.ShapeDtypeStruct((items, dim), dtype)
    scratch = [
        pltpu.SMEM((3 * slots,), jnp.int32),
        pltpu.VMEM((slots, piece_rows, dim), jnp.bfloat16),
        pltpu.VMEM((slots, LOG_ROWS, dim), jnp.bfloat16),
        pltpu.VMEM((dim, items), jnp.float32),
    ]
    sems = [pltpu.SemaphoreType.DMA((slots,))] * 2
    if last:
        outs = (
            right,
            jax.ShapeDtypeStruct((n_col // 2, items, dim), jnp.bfloat16),
            jax.ShapeDtypeStruct((n_col // 2, items, dim), jnp.float32),
        )
        scratch += [
            pltpu.VMEM((n_col * items, dim), jnp.float32),
            pltpu.VMEM((slots, piece_rows, dim), jnp.float32),
        ]
        sems += [pltpu.SemaphoreType.DMA((slots,))]
    else:
        outs = (right, jax.ShapeDtypeStruct((slots, piece_rows, dim), jnp.float32))
    return pl.pallas_call(
        functools.partial(tile_kernel, distance, n_col, tuple(earlier), last),
        out_shape=outs,
        in_specs=[vmem_spec] * 3
        + [any_spec] * n_col
        + [vmem_spec]
        + [any_spec] * (len(earlier) + 1),
        out_specs=tuple(vmem_spec for _ in outs),
        scratch_shapes=scratch + sems,
        compiler_params=pltpu.CompilerParams(vmem_limit_bytes=24 * MIB),
    )(listing, *tiles, *rows, window, *earlier.values(), after)


def shards(embedding, accumulator, popularity, cooccur, pair_list, live_count):
    items = embedding.shape[0]
    n_col = lax.axis_size("col")
    listing = jnp.transpose(pair_list, (0, 3, 1, 2)).reshape(1, -1)
    listing = jnp.concatenate([listing, live_count], axis=1)
    listing = jnp.pad(listing, ((0, 7), (0, LANES - listing.shape[1])))
    message = pack(embedding, popularity)
    reach = min(8, lax.axis_size("row"))
    windows = {0: message, 1: shifted(message, "row", -1)}
    if reach == 4:
        windows[3] = shifted(message, "row", -3)
        below = lax.ppermute(message, "row", [(3, 1)])
    tiles = fetch(listing, cooccur)
    rows = {0: message}
    bit = n_col // 2
    while bit:
        for place, block in list(rows.items()):
            if place:
                block, windows[1], tiles = lax.optimization_barrier((block, windows[1], tiles))
                rows[place ^ bit] = flipped(block, "col", bit)
            else:
                rows[place ^ bit] = flipped(block, "col", bit)
        bit //= 2
    rows = [rows[place] for place in range(n_col)]
    if reach == 4:
        windows[2] = below + lax.ppermute(windows[1], "row", [(1, 0)])
    else:
        for distance in range(2, reach):
            windows[distance] = shifted(message, "row", -distance)
    right, earlier, received = {}, {}, {}
    order = [1, 0, *range(reach - 1, 1, -1)]
    for distance in order:
        last = distance == order[-1]
        done = run_tiles(
            distance,
            listing,
            tiles,
            rows,
            windows[distance],
            earlier,
            last,
            jnp.bfloat16 if distance else jnp.float32,
            received[1] if last else message,
        )
        right[distance], earlier[distance] = done[:2]
        if distance:
            received[distance] = shifted(right[distance], "row", distance)
    send, keep = done[1], done[2]
    keep = [keep[place] for place in range(n_col // 2)]
    ties = [received[distance] for distance in order[2:-1]]
    first, ties = lax.optimization_barrier((send[0], ties))
    got = [
        jnp.concatenate([flipped(part, "col", 1) for part in jnp.split(block, PARTS)])
        for block in [first, *[send[place] for place in range(1, n_col // 2)]]
    ]
    keep = [mine + got[place].astype(jnp.float32) for place, mine in enumerate(keep)]
    bit = 2
    while bit < n_col:
        sent = [keep[place].astype(jnp.bfloat16) for place in range(1, len(keep), 2)]
        keep = [
            keep[2 * place] + flipped(block, "col", bit).astype(jnp.float32)
            for place, block in enumerate(sent)
        ]
        bit *= 2
    gradient = right[0] + keep[0]
    for block in (received[1], *ties, received[order[-1]]):
        gradient = gradient + block.astype(jnp.float32)
    new_accumulator = accumulator + gradient * gradient
    new_embedding = embedding - LEARN_RATE * gradient / jnp.sqrt(new_accumulator)
    return (new_embedding, new_accumulator)


def solution(mesh):
    in_specs = (
        P(("parts", "row", "col"), None),
        P(("parts", "row", "col"), None),
        P(("parts", "row", "col")),
        P(("parts", "row"), "col", None, None, None),
        P(("parts", "row"), "col", None, None),
        P(("parts", "row"), "col"),
    )
    out_specs = (P(("parts", "row", "col"), None), P(("parts", "row", "col"), None))
    return jax.shard_map(shards, mesh=mesh, in_specs=in_specs, out_specs=out_specs, check_vma=False)
```

```python
import functools
import math

import jax
import jax.numpy as jnp
from jax import lax
from jax.experimental import pallas as pl
from jax.experimental.pallas import tpu as pltpu
from jax.sharding import PartitionSpec as P

LOG_SHIFT = 4.0
LEARN_RATE = 0.5
LANES = 128
LOG_ROWS = 16
CHUNK = 1024
STRIP = 32
MIB = 1 << 20
PARTS = 1


def shifted(array, axis, by):
    count = lax.axis_size(axis)
    pairs = [(i, i + by) for i in range(count) if 0 <= i + by < count]
    return lax.ppermute(array, axis, pairs)


def flipped(array, axis, bit):
    count = lax.axis_size(axis)
    return lax.ppermute(array, axis, [(i, i ^ bit) for i in range(count)])


def pack_kernel(embedding, popularity, message):
    items = embedding.shape[0]
    message[:items] = embedding[...].astype(jnp.bfloat16)
    logs = jnp.log(popularity[...].astype(jnp.float32))
    message[items:] = jnp.concatenate([logs, jnp.zeros_like(logs)], axis=0).astype(jnp.bfloat16)


def pack(embedding, popularity):
    items, dim = embedding.shape
    return pl.pallas_call(
        pack_kernel,
        out_shape=jax.ShapeDtypeStruct((items + LOG_ROWS, dim), jnp.bfloat16),
        in_specs=[pl.BlockSpec(memory_space=pltpu.VMEM)] * 2,
        out_specs=pl.BlockSpec(memory_space=pltpu.VMEM),
        compiler_params=pltpu.CompilerParams(vmem_limit_bytes=4 * MIB),
    )(embedding, popularity.reshape(items // LANES, LANES))


def fetch_kernel(listing, cooccur, gains, targets):
    slots, piece_rows, items = gains.shape
    scale = 1.0 / math.sqrt(items)
    n_live = listing[0, 3 * slots]

    @pl.loop(0, slots)
    def _(slot):
        @pl.when(slot < n_live)
        def _():
            @pl.loop(0, piece_rows // STRIP)
            def _(strip):
                rows = pl.ds(pl.multiple_of(strip * STRIP, STRIP), STRIP)
                count = cooccur[0, 0, slot, rows, :].astype(jnp.float32)
                clipped = jnp.maximum(count, 1.0)
                root = clipped * lax.rsqrt(clipped)
                gain = 0.1 * scale + (0.25 * scale) * root
                gains[slot, rows, :] = jnp.where(count > 0, gain, 0.0)
                targets[slot, rows, :] = jnp.log(clipped)


def fetch(listing, cooccur):
    _, _, slots, piece_rows, items = cooccur.shape
    shape = jax.ShapeDtypeStruct((slots, piece_rows, items), jnp.float32)
    vmem_spec = pl.BlockSpec(memory_space=pltpu.VMEM)
    return pl.pallas_call(
        fetch_kernel,
        out_shape=(shape, shape),
        in_specs=[vmem_spec, vmem_spec],
        out_specs=(vmem_spec, vmem_spec),
        compiler_params=pltpu.CompilerParams(vmem_limit_bytes=24 * MIB),
    )(listing, cooccur)


def tile_kernel(distance, n_col, earlier, last, *refs):
    refs = list(refs)
    take = lambda count: [refs.pop(0) for _ in range(count)]
    listing, gains, targets = take(3)
    row_refs = take(n_col)
    (window,) = take(1)
    prev = take(len(earlier))
    take(1)
    (right_out,) = take(1)
    left_outs = take(2 if last else 1)
    pairs, row_vecs, row_logs, right_acc = take(4)
    if last:
        left_acc, pieces = take(2)
    vec_sem, log_sem = take(2)
    if last:
        (piece_sem,) = take(1)
    slots, piece_rows, items = gains.shape
    me = lax.axis_index("col")
    n_live = listing[0, 3 * slots]
    for index in range(3 * slots):
        pairs[index] = listing[0, index]
    scale = 1.0 / math.sqrt(items)

    def listed(slot):
        return jnp.logical_and(slot < n_live, pairs[slots + slot] == distance)

    def row_copies(slot, source):
        first = pl.multiple_of(pairs[2 * slots + slot] * piece_rows, piece_rows)
        return (
            pltpu.make_async_copy(
                source.at[pl.ds(first, piece_rows)], row_vecs.at[slot], vec_sem.at[slot]
            ),
            pltpu.make_async_copy(
                source.at[pl.ds(items, LOG_ROWS)], row_logs.at[slot], log_sem.at[slot]
            ),
        )

    def piece_copy(slot, source):
        return pltpu.make_async_copy(source.at[slot], pieces.at[slot], piece_sem.at[slot])

    for slot in range(slots):

        @pl.when(listed(slot))
        def _():
            place = jnp.bitwise_xor(pairs[slot], me)
            for index in range(n_col):

                @pl.when(place == index)
                def _():
                    for copy in row_copies(slot, row_refs[index]):
                        copy.start()

        if last:
            for source, index in zip(prev, earlier):

                @pl.when(jnp.logical_and(slot < n_live, pairs[slots + slot] == index))
                def _():
                    piece_copy(slot, source).start()

    any_listed = listed(0)
    for slot in range(1, slots):
        any_listed = jnp.logical_or(any_listed, listed(slot))

    @pl.when(any_listed)
    def _():
        right_acc[...] = jnp.zeros_like(right_acc)

    if last:
        left_acc[...] = jnp.zeros_like(left_acc)

    def add_left(slot, value):
        place = jnp.bitwise_xor(pairs[slot], me)
        first = place * items + pairs[2 * slots + slot] * piece_rows
        view = pl.ds(pl.multiple_of(first, piece_rows), piece_rows)
        left_acc[view, :] += value

    def one_tile(slot):
        for copy in row_copies(slot, row_refs[0]):
            copy.wait()
        piece = row_vecs[slot]
        piece_t = piece.T
        group = pairs[2 * slots + slot] * (piece_rows // LANES)
        logs = row_logs[slot]
        places = lax.broadcasted_iota(jnp.int32, (LOG_ROWS, LANES), 0)
        log_rows = []
        for part in range(piece_rows // LANES):
            chosen = jnp.where(places == group + part, 1.0, 0.0).astype(jnp.bfloat16)
            log_rows.append(
                lax.dot_general(
                    logs, chosen, (((0,), (0,)), ((), ())), preferred_element_type=jnp.float32
                )
            )
        row_term = jnp.concatenate(log_rows, axis=0) - LOG_SHIFT
        row_term = jnp.concatenate([row_term] * (CHUNK // LANES), axis=1)
        col_logs = window[items:, :].astype(jnp.float32)
        left = jnp.zeros((piece_rows, piece.shape[1]), jnp.float32)
        for chunk in range(items // CHUNK):
            cols = slice(chunk * CHUNK, (chunk + 1) * CHUNK)
            block = window[cols, :]
            per = CHUNK // LANES
            col_term = jnp.concatenate(
                [col_logs[chunk * per + i : chunk * per + i + 1] for i in range(per)], axis=1
            )
            scores = lax.dot_general(
                piece, block, (((1,), (1,)), ((), ())), preferred_element_type=jnp.float32
            )
            gain = gains[slot, :, cols]
            misfit = (scores + row_term) + (col_term - targets[slot, :, cols])
            unseen = (0.5 * scale) * jnp.tanh(0.5 * misfit) + 0.5 * scale
            weights = jnp.where(gain > 0, gain * misfit, unseen).astype(jnp.bfloat16)
            left = left + jnp.dot(weights, block, preferred_element_type=jnp.float32)
            right_acc[:, cols] += jnp.dot(piece_t, weights, preferred_element_type=jnp.float32)
        if last:
            add_left(slot, left)
        else:
            left_outs[0][slot] = left

    @pl.loop(0, slots)
    def _(slot):
        @pl.when(listed(slot))
        def _():
            one_tile(slot)

    @pl.when(any_listed)
    def _():
        right_out[...] = right_acc[...].T.astype(right_out.dtype)

    @pl.when(jnp.logical_not(any_listed))
    def _():
        right_out[...] = jnp.zeros_like(right_out)

    if last:

        @pl.loop(0, slots)
        def _(slot):
            @pl.when(jnp.logical_and(slot < n_live, jnp.logical_not(listed(slot))))
            def _():
                piece_copy(slot, prev[0]).wait()
                add_left(slot, pieces[slot])

        for index in range(n_col):
            block = left_acc[index * items : (index + 1) * items, :]
            if index % 2:
                left_outs[0][index // 2] = block.astype(jnp.bfloat16)
            else:
                left_outs[1][index // 2] = block


def run_tiles(distance, listing, tiles, rows, window, earlier, last, dtype, after):
    slots, piece_rows, items = tiles[0].shape
    dim = window.shape[1]
    n_col = len(rows)
    any_spec = pl.BlockSpec(memory_space=pl.ANY)
    vmem_spec = pl.BlockSpec(memory_space=pltpu.VMEM)
    right = jax.ShapeDtypeStruct((items, dim), dtype)
    scratch = [
        pltpu.SMEM((3 * slots,), jnp.int32),
        pltpu.VMEM((slots, piece_rows, dim), jnp.bfloat16),
        pltpu.VMEM((slots, LOG_ROWS, dim), jnp.bfloat16),
        pltpu.VMEM((dim, items), jnp.float32),
    ]
    sems = [pltpu.SemaphoreType.DMA((slots,))] * 2
    if last:
        outs = (
            right,
            jax.ShapeDtypeStruct((n_col // 2, items, dim), jnp.bfloat16),
            jax.ShapeDtypeStruct((n_col // 2, items, dim), jnp.float32),
        )
        scratch += [
            pltpu.VMEM((n_col * items, dim), jnp.float32),
            pltpu.VMEM((slots, piece_rows, dim), jnp.float32),
        ]
        sems += [pltpu.SemaphoreType.DMA((slots,))]
    else:
        outs = (right, jax.ShapeDtypeStruct((slots, piece_rows, dim), jnp.float32))
    return pl.pallas_call(
        functools.partial(tile_kernel, distance, n_col, tuple(earlier), last),
        out_shape=outs,
        in_specs=[vmem_spec] * 3
        + [any_spec] * n_col
        + [vmem_spec]
        + [any_spec] * (len(earlier) + 1),
        out_specs=tuple(vmem_spec for _ in outs),
        scratch_shapes=scratch + sems,
        compiler_params=pltpu.CompilerParams(vmem_limit_bytes=24 * MIB),
    )(listing, *tiles, *rows, window, *earlier.values(), after)


def shards(embedding, accumulator, popularity, cooccur, pair_list, live_count):
    items = embedding.shape[0]
    n_col = lax.axis_size("col")
    listing = jnp.transpose(pair_list, (0, 3, 1, 2)).reshape(1, -1)
    listing = jnp.concatenate([listing, live_count], axis=1)
    listing = jnp.pad(listing, ((0, 7), (0, LANES - listing.shape[1])))
    message = pack(embedding, popularity)
    reach = min(8, lax.axis_size("row"))
    windows = {0: message, 1: shifted(message, "row", -1)}
    if reach == 4:
        windows[3] = shifted(message, "row", -3)
        below = lax.ppermute(message, "row", [(3, 1)])
    tiles = fetch(listing, cooccur)
    rows = {0: message}
    bit = n_col // 2
    while bit:
        for place, block in list(rows.items()):
            if place:
                block, windows[1], tiles = lax.optimization_barrier((block, windows[1], tiles))
                rows[place ^ bit] = flipped(block, "col", bit)
            else:
                rows[place ^ bit] = flipped(block, "col", bit)
        bit //= 2
    rows = [rows[place] for place in range(n_col)]
    if reach == 4:
        windows[2] = below + lax.ppermute(windows[1], "row", [(1, 0)])
    else:
        for distance in range(2, reach):
            windows[distance] = shifted(message, "row", -distance)
    right, earlier, received = {}, {}, {}
    order = [1, 0, *range(reach - 1, 1, -1)]
    for distance in order:
        last = distance == order[-1]
        done = run_tiles(
            distance,
            listing,
            tiles,
            rows,
            windows[distance],
            earlier,
            last,
            jnp.bfloat16 if distance else jnp.float32,
            received[1] if last else message,
        )
        right[distance], earlier[distance] = done[:2]
        if distance:
            received[distance] = shifted(right[distance], "row", distance)
    send, keep = done[1], done[2]
    keep = [keep[place] for place in range(n_col // 2)]
    ties = [received[distance] for distance in order[2:-1]]
    first, ties = lax.optimization_barrier((send[0], ties))
    got = [
        jnp.concatenate([flipped(part, "col", 1) for part in jnp.split(block, PARTS)])
        for block in [first, *[send[place] for place in range(1, n_col // 2)]]
    ]
    keep = [mine + got[place].astype(jnp.float32) for place, mine in enumerate(keep)]
    bit = 2
    while bit < n_col:
        sent = [keep[place].astype(jnp.bfloat16) for place in range(1, len(keep), 2)]
        keep = [
            keep[2 * place] + flipped(block, "col", bit).astype(jnp.float32)
            for place, block in enumerate(sent)
        ]
        bit *= 2
    gradient = right[0] + keep[0]
    for block in (received[1], *ties, received[order[-1]]):
        gradient = gradient + block.astype(jnp.float32)
    new_accumulator = accumulator + gradient * gradient
    new_embedding = embedding - LEARN_RATE * gradient * lax.rsqrt(new_accumulator)
    return (new_embedding, new_accumulator)


def solution(mesh):
    in_specs = (
        P(("parts", "row", "col"), None),
        P(("parts", "row", "col"), None),
        P(("parts", "row", "col")),
        P(("parts", "row"), "col", None, None, None),
        P(("parts", "row"), "col", None, None),
        P(("parts", "row"), "col"),
    )
    out_specs = (P(("parts", "row", "col"), None), P(("parts", "row", "col"), None))
    return jax.shard_map(shards, mesh=mesh, in_specs=in_specs, out_specs=out_specs, check_vma=False)
```
